128 devices in a mesh: seg: 8 (over z, x_hi), lines: 16 (over x_lo, y, core).
Axes of the slice: x: 4 (x_hi: 2, x_lo: 2; x = x_hi * 2 + x_lo), y: 4, z: 4, core: 2. Of those that a mesh axis runs over, the one named last changes fastest.
Arguments:
- left_features: bfloat16 [64, 8192, 128], P('lines', 'seg'), may hold values from -400 to 400
- right_features: bfloat16 [64, 8192, 128], P('lines', 'seg'), may hold values from -6 to 6
- conv_weight: bfloat16 [3, 3, 3, 128, 128], replicated, may hold values from -0.1875 to 0.1875
- conv_bias: float32 [3, 128], replicated, may hold values from -3 to 3
Outputs:
- refined: bfloat16 [64, 8192, 128], P('lines', 'seg')
- disparity: float32 [64, 8192], P('lines', 'seg')
The draws below stay inside these ranges and needn't reach their ends.
All inputs are finite; a program needn't handle non-finite values.
Results may differ from the reference program's by a relative error of at most 0.006.
Values may be sent and summed in bfloat16 or wider, within the bound.
A program may use at most 128 MiB of HBM per device.

```python
import math
import jax
import jax.numpy as jnp
from jax import lax

C = 128
DISP = 1024
SWEEPS = 2
LAYERS = 3
SEG = 1024
LINES = 64
PIXELS = 8192


def stereo_pair(key):
    base = jax.random.fold_in(key, 7103)
    right_key, left_key = jax.random.split(base, 2)
    shape = (LINES, PIXELS, C)
    right = jnp.clip(jax.random.normal(right_key, shape, jnp.float32), -6.0, 6.0)
    left = jnp.clip(jax.random.normal(left_key, shape, jnp.float32), -6.0, 6.0)
    return (jnp.clip(left, -400.0, 400.0), right)


def draw_left_features(key, part):
    return stereo_pair(key)[0].astype(jnp.bfloat16)


def draw_right_features(key, part):
    return stereo_pair(key)[1].astype(jnp.bfloat16)


def centred(own_key, dims, scale, reach, held_as=jnp.bfloat16):
    entries = scale * jax.random.normal(own_key, dims, jnp.float32)
    return jnp.clip(entries, min=-reach, max=reach).astype(held_as)


def setup_inputs(seed: int = 0) -> dict:
    streams_of = jax.random.split(jax.random.key(seed), 5)
    return {
        "left_features": draw_left_features(jax.random.fold_in(streams_of[4], 71), 0),
        "right_features": draw_right_features(jax.random.fold_in(streams_of[4], 71), 0),
        "conv_weight": centred(streams_of[2], (LAYERS, 3, 3, C, C), (9 * C) ** -0.5, 0.1875),
        "conv_bias": centred(streams_of[3], (LAYERS, C), 0.5, 3.0, jnp.float32),
    }


NEG = -1e+30

def merge_parts(first_part, second_part):
    maxima = jnp.maximum(first_part[0], second_part[0])
    totals = first_part[1] * jnp.exp(first_part[0] - maxima) + second_part[1] * jnp.exp(second_part[0] - maxima)
    return (maxima, totals)

def potentials(maxima, totals):
    live = totals > 0
    return jnp.where(live, -(maxima + jnp.log(jnp.where(live, totals, 1.0))), 0.0)

def band_scores(left_blk, right_win, offset, band_reach, valid_from):
    scores = jnp.einsum('lrc,lkc->lrk', left_blk.astype(jnp.float32), right_win.astype(jnp.float32), precision=lax.Precision.HIGHEST)
    scores = scores * (1.0 / math.sqrt(left_blk.shape[2]))
    row_ids = lax.broadcasted_iota(jnp.int32, scores.shape, 1)
    col_ids = lax.broadcasted_iota(jnp.int32, scores.shape, 2)
    inside = (col_ids > row_ids) & (col_ids <= row_ids + band_reach) & (col_ids + offset >= valid_from)
    return (scores, inside, row_ids, col_ids)

def column_partials(left_side, right_ext, row_pot, band_reach, valid_from, block_rows):
    lines_here, seg_len = (left_side.shape[0], left_side.shape[1])
    window = block_rows + band_reach
    maxima = jnp.full((lines_here, seg_len + band_reach), NEG, jnp.float32)
    totals = jnp.zeros((lines_here, seg_len + band_reach), jnp.float32)
    for offset in range(0, seg_len, block_rows):
        scores, inside, row_ids, col_ids = band_scores(left_side[:, offset:offset + block_rows], right_ext[:, offset:offset + window], offset, band_reach, valid_from)
        shifted = jnp.where(inside, scores + row_pot[:, offset:offset + block_rows, None], NEG)
        block_max = lax.optimization_barrier(jnp.max(shifted, axis=1))
        block_sum = lax.optimization_barrier(jnp.sum(jnp.where(inside, jnp.exp(shifted - block_max[:, None, :]), 0.0), axis=1))
        merged = merge_parts((maxima[:, offset:offset + window], totals[:, offset:offset + window]), (block_max, block_sum))
        maxima = maxima.at[:, offset:offset + window].set(merged[0])
        totals = totals.at[:, offset:offset + window].set(merged[1])
    return (maxima, totals)

def row_potentials(left_side, right_ext, col_pot, band_reach, valid_from, block_rows):
    seg_len = left_side.shape[1]
    window = block_rows + band_reach
    pieces = []
    for offset in range(0, seg_len, block_rows):
        scores, inside, row_ids, col_ids = band_scores(left_side[:, offset:offset + block_rows], right_ext[:, offset:offset + window], offset, band_reach, valid_from)
        shifted = jnp.where(inside, scores + col_pot[:, None, offset:offset + window], NEG)
        row_max = lax.optimization_barrier(jnp.max(shifted, axis=2))
        row_sum = lax.optimization_barrier(jnp.sum(jnp.where(inside, jnp.exp(shifted - row_max[:, :, None]), 0.0), axis=2))
        pieces.append(-(row_max + jnp.log(row_sum)))
    return jnp.concatenate(pieces, axis=1)

def transport(left_side, right_ext, row_pot, col_pot, band_reach, valid_from, block_rows):
    seg_len = left_side.shape[1]
    window = block_rows + band_reach
    matched_parts = []
    disparity_parts = []
    for offset in range(0, seg_len, block_rows):
        right_win = right_ext[:, offset:offset + window]
        scores, inside, row_ids, col_ids = band_scores(left_side[:, offset:offset + block_rows], right_win, offset, band_reach, valid_from)
        weights = jnp.where(inside, jnp.exp(scores + row_pot[:, offset:offset + block_rows, None] + col_pot[:, None, offset:offset + window]), 0.0)
        distance = (row_ids - col_ids + band_reach).astype(jnp.float32)
        disparity_parts.append(lax.optimization_barrier(jnp.sum(weights * distance, axis=2)))
        weights_low = weights.astype(jnp.bfloat16)
        matched_parts.append(jnp.einsum('lrk,lkc->lrc', weights_low.astype(jnp.float32), right_win.astype(jnp.float32), precision=lax.Precision.HIGHEST))
    return (jnp.concatenate(matched_parts, axis=1), jnp.concatenate(disparity_parts, axis=1))

def conv_layer(state, padded, kernel, bias):
    height, width, channels = state.shape
    total = jnp.zeros((height * width, channels), jnp.float32)
    for row_tap in range(3):
        for col_tap in range(3):
            shifted = padded[row_tap:row_tap + height, col_tap:col_tap + width].reshape(height * width, channels)
            total = total + jnp.dot(shifted, kernel[row_tap, col_tap], preferred_element_type=jnp.float32)
    updated = state.astype(jnp.float32) + jax.nn.relu(total.reshape(state.shape) + bias)
    return updated.astype(jnp.bfloat16)

def one_line(line_pair):
    left_side = line_pair[0][None]
    right_side = line_pair[1][None]
    channels = left_side.shape[2]
    block_rows = min(512, SEG)
    right_ext = jnp.concatenate([jnp.zeros((1, DISP, channels), jnp.bfloat16), right_side], axis=1)
    row_pot = jnp.zeros((1, PIXELS), jnp.float32)
    col_pot = jnp.zeros((1, PIXELS + DISP), jnp.float32)
    for sweep_index in range(SWEEPS):
        maxima, totals = column_partials(left_side, right_ext, row_pot, DISP, DISP, block_rows)
        col_pot = potentials(maxima, totals)
        row_pot = row_potentials(left_side, right_ext, col_pot, DISP, DISP, block_rows)
    matched, disparity = transport(left_side, right_ext, row_pot, col_pot, DISP, DISP, block_rows)
    residual = (matched - left_side.astype(jnp.float32)).astype(jnp.bfloat16)
    return (residual[0], disparity[0])

def reference(left_features, right_features, conv_weight, conv_bias):
    residual, disparity = lax.map(one_line, (left_features, right_features))
    state = residual
    for layer in range(LAYERS):
        padded = jnp.pad(state, ((1, 1), (1, 1), (0, 0)))
        state = conv_layer(state, padded, conv_weight[layer], conv_bias[layer])
    return (state, disparity)
```

```python
import functools
import math

import jax
import jax.numpy as jnp
from jax import lax
from jax.experimental import pallas as pl
from jax.experimental.pallas import tpu as pltpu
from jax.sharding import PartitionSpec as P

NEG = -1e30
LOG2E = 1.4426950408889634
PAD = 16
REACH = 3
MESH = pl.DeviceIdType.MESH
F32 = jnp.float32
BF16 = jnp.bfloat16


def nt_dot(a, b):
    return lax.dot_general(a, b, (((1,), (1,)), ((), ())), preferred_element_type=F32)


def groups(x):
    return x.reshape(x.shape[0] // 8, 8, x.shape[1])


def body(
    shape, left_hbm, right_hbm, w_hbm, bias_ref, out_ref, disp_ref,
    left_v, right_v, tcol, s_ref, own_mt, halo_mt, own_in, halo_in, c1, c2acc,
    own_c2, halo_c2, own_c2_in, halo_c2_in, w_v, wbig, x0, x1, x2, y_ref,
    load_sem, wsem, halo_ss, halo_rs, mt_ss, mt_rs, c2_ss, c2_rs, ln_ss, ln_rs,
):
    segs, line_devs, lines, n, blk, chans, layers = shape
    nblk = n // blk
    win = n + blk
    wide = n + 2 * PAD
    scale = LOG2E / math.sqrt(chans)
    seg = lax.axis_index("seg")
    me = lax.axis_index("lines")
    core = lax.rem(me, 2)
    mate = me + 1 - 2 * core
    cross = me - 1 + 2 * core
    has_l = seg > 0
    has_r = seg < segs - 1
    has_x = (cross >= 0) & (cross < line_devs)

    def dev(ds, ln):
        return {"seg": seg + ds, "lines": ln}

    def line_of(u):
        return u + core * (lines - 1 - 2 * u)

    def remote(src, dst, ss, rs, where):
        return pltpu.make_async_remote_copy(
            src_ref=src, dst_ref=dst, send_sem=ss, recv_sem=rs, device_id=where, device_id_type=MESH
        )

    barrier = pltpu.get_barrier_semaphore()
    peers = []
    for ds, side in ((-1, has_l), (1, has_r)):
        peers += [(side, dev(ds, me)), (side, dev(ds, mate)), (side & has_x, dev(ds, cross))]
    peers += [(me >= 0, dev(0, mate)), (has_x, dev(0, cross))]
    for cond, where in peers:
        @pl.when(cond)
        def _():
            pl.semaphore_signal(barrier, inc=1, device_id=where, device_id_type=MESH)

    def load(u, which):
        src = (left_hbm, right_hbm)[which].at[line_of(u)]
        dst = left_v.at[u] if which == 0 else right_v.at[u, pl.ds(n, n)]
        return pltpu.make_async_copy(src, dst, load_sem.at[u, which])

    for u in range(lines):
        load(u, 0).start()
        load(u, 1).start()
    wload = pltpu.make_async_copy(w_hbm, w_v, wsem)
    wload.start()

    pl.semaphore_wait(barrier, sum(cond.astype(jnp.int32) for cond, _ in peers))

    def halo_copy(u):
        return remote(
            right_hbm.at[line_of(u)], right_v.at[u, pl.ds(0, n)], halo_ss.at[u], halo_rs.at[u],
            dev(1, me),
        )

    @pl.when(has_r)
    def _():
        for u in range(lines):
            halo_copy(u).start()

    def mt_up(u):
        return remote(own_mt.at[u], halo_in.at[u], mt_ss.at[u, 0], mt_rs.at[u, 0], dev(1, me))

    def mt_down(u):
        return remote(halo_mt.at[u], own_in.at[u], mt_ss.at[u, 1], mt_rs.at[u, 1], dev(-1, me))

    def c2_up(u):
        return remote(own_c2.at[u], halo_c2_in.at[u], c2_ss.at[u, 0], c2_rs.at[u, 0], dev(1, me))

    def c2_down(u):
        return remote(halo_c2.at[u], own_c2_in.at[u], c2_ss.at[u, 1], c2_rs.at[u, 1], dev(-1, me))

    def line_routes():
        routes = []
        for u in range(lines):
            routes.append((u, u + REACH, None, 0, me))
            if u < REACH:
                routes.append((u, REACH - 1 - u, has_x, 1, cross))
            if u >= lines - REACH:
                routes.append((u, 2 * lines + REACH - 1 - u, None, 2, mate))
        return routes

    def line_copies(u_pick):
        copies = []
        for u, slot, cond, to, ln in line_routes():
            if u_pick is not None and u != u_pick:
                continue
            mine = u + REACH
            cond = me >= 0 if cond is None else cond
            if to:
                copies.append((cond, cond, remote(
                    x0.at[mine, pl.ds(PAD, n)], x0.at[slot, pl.ds(PAD, n)],
                    ln_ss.at[u, to, 0], ln_rs.at[slot, 0], dev(0, ln))))
            copies.append((cond & has_r, cond & has_l, remote(
                x0.at[mine, pl.ds(n, PAD)], x0.at[slot, pl.ds(0, PAD)],
                ln_ss.at[u, to, 1], ln_rs.at[slot, 1], dev(1, ln))))
            copies.append((cond & has_l, cond & has_r, remote(
                x0.at[mine, pl.ds(PAD, PAD)], x0.at[slot, pl.ds(n + PAD, PAD)],
                ln_ss.at[u, to, 2], ln_rs.at[slot, 2], dev(-1, ln))))
        return copies

    e_ids = lax.broadcasted_iota(jnp.int32, (2 * n, chans), 0)
    lane = lax.broadcasted_iota(jnp.int32, (2 * n, chans), 1)
    t = n - e_ids
    low = t & 7
    tcol[...] = jnp.where(
        lane == 0, 1, jnp.where(lane == 1, t - low, jnp.where(lane == 2, low, 0))
    ).astype(F32).astype(BF16)

    @pl.when(jnp.logical_not(has_l))
    def _():
        right_v[:, 0:n, :] = jnp.zeros((lines, n, chans), BF16)
        halo_in[:, 0:1, :] = jnp.full((lines, 1, n), NEG, F32)
        halo_in[:, 1:2, :] = jnp.zeros((lines, 1, n), F32)
        halo_c2_in[...] = jnp.zeros((lines, 1, n), F32)
        x0[:, 0:PAD, :] = jnp.zeros((lines + 2 * REACH, PAD, chans), BF16)

    @pl.when(jnp.logical_not(has_r))
    def _():
        own_in[:, 0:1, :] = jnp.full((lines, 1, n), NEG, F32)
        own_in[:, 1:2, :] = jnp.zeros((lines, 1, n), F32)
        own_c2_in[...] = jnp.zeros((lines, 1, n), F32)
        x0[:, n + PAD : wide, :] = jnp.zeros((lines + 2 * REACH, PAD, chans), BF16)

    @pl.when(jnp.logical_not(has_x))
    def _():
        x0[0:REACH] = jnp.zeros((REACH, wide, chans), BF16)

    y_ref[:, 0:8, :] = jnp.zeros((6, 8, chans), F32)
    y_ref[:, 8 + wide : 16 + wide, :] = jnp.zeros((6, 8, chans), F32)

    il = lax.broadcasted_iota(jnp.int32, (blk, blk), 0)
    jl = lax.broadcasted_iota(jnp.int32, (blk, blk), 1)

    def partial_lse(u, own):
        base = n if own else 0
        dst = own_mt if own else halo_mt
        for c in range(nblk):
            cols = right_v[u, base + c * blk : base + (c + 1) * blk, :]
            run_m = jnp.full((8, blk), NEG, F32)
            run_t = jnp.zeros((8, blk), F32)
            for r in range(c, nblk) if own else range(c + 1):
                s = nt_dot(left_v[u, r * blk : (r + 1) * blk, :], cols) * scale
                if r == c:
                    s = jnp.where(jl <= il if own else jl > il, s, NEG)
                at = base + (c - r) * blk
                s_ref[u, r, :, at : at + blk] = s
                g = groups(s)
                m = jnp.maximum(run_m, jnp.max(g, axis=0))
                run_t = run_t * jnp.exp2(run_m - m) + jnp.sum(jnp.exp2(g - m[None]), axis=0)
                run_m = m
            m = jnp.max(run_m, axis=0, keepdims=True)
            dst[u, 0:1, c * blk : (c + 1) * blk] = m
            dst[u, 1:2, c * blk : (c + 1) * blk] = jnp.sum(
                run_t * jnp.exp2(run_m - m), axis=0, keepdims=True
            )

    def col_pot(a, b):
        m = jnp.maximum(a[0:1], b[0:1])
        tot = a[1:2] * jnp.exp2(a[0:1] - m) + b[1:2] * jnp.exp2(b[0:1] - m)
        return -(m + jnp.log(tot) * LOG2E)

    sub = blk // 2

    def row_pass(u):
        own = col_pot(own_mt[u], own_in[u])
        halo = jnp.where(has_l, col_pot(halo_mt[u], halo_in[u]), NEG)
        c1[:, n : 2 * n] = jnp.broadcast_to(own, (8, n))
        c1[:, 0:n] = jnp.broadcast_to(halo, (8, n))
        c2acc[...] = jnp.zeros((8, 2 * n), F32)

        def step(k, carry):
            r = k // 2
            rows = pl.multiple_of(lax.rem(k, 2) * sub, sub)
            at = pl.multiple_of(r * blk, blk)
            pot = c1[:, pl.ds(at, win)][None]
            total = jnp.zeros((8, win), F32)
            piece = sub // 4
            for p in range(4):
                here = pl.ds(rows + p * piece, piece)
                sc = groups(s_ref[u, r, here, :]) + pot
                k_el = jnp.exp2(sc - jnp.max(sc, axis=2, keepdims=True))
                s_ref[u, r, here, :] = k_el.reshape(piece, win)
                inv = 1.0 / jnp.sum(k_el, axis=2, keepdims=True)
                total = total + jnp.sum(k_el * inv, axis=0)
            c2acc[:, pl.ds(at, win)] += total
            return carry

        lax.fori_loop(0, 2 * nblk, step, 0)
        halo_c2[u] = jnp.sum(c2acc[:, 0:n], axis=0, keepdims=True)
        own_c2[u] = jnp.sum(c2acc[:, n : 2 * n], axis=0, keepdims=True)

    def transport(u):
        c1[:, n : 2 * n] = jnp.broadcast_to(1.0 / (own_c2[u] + own_c2_in[u]), (8, n))
        c1[:, 0:n] = jnp.broadcast_to(
            jnp.where(has_l, 1.0 / (halo_c2[u] + halo_c2_in[u]), 0.0), (8, n)
        )
        ln = line_of(u)

        def step(r, carry):
            at = pl.multiple_of(r * blk, blk)
            q = groups(s_ref[u, r]) * c1[:, pl.ds(at, win)][None]
            q = q.reshape(blk, win).astype(BF16)
            rhs = jnp.concatenate([right_v[u, pl.ds(at, win), :], tcol[pl.ds(at, win), :]], axis=1)
            o = jnp.dot(q, rhs, preferred_element_type=F32)
            matched = o[:, :chans] / o[:, chans : chans + 1]
            x0[u + REACH, pl.ds(PAD + at, blk), :] = (
                matched - left_v[u, pl.ds(at, blk), :].astype(F32)
            ).astype(BF16)
            rowed = jnp.transpose(o[:, chans:])
            ids = (lax.broadcasted_iota(jnp.int32, (1, blk), 1) + at).astype(F32)
            disp_ref[pl.ds(ln, 1), pl.ds(at, blk)] = ids + (rowed[1:2] + rowed[2:3]) / rowed[0:1]
            return carry

        lax.fori_loop(0, nblk, step, 0)

    def own_step(u, carry):
        load(u, 0).wait()
        load(u, 1).wait()
        partial_lse(u, True)

        @pl.when(has_r)
        def _():
            mt_up(u).start()

        return carry

    lax.fori_loop(0, lines, own_step, 0)

    wload.wait()
    wbig[...] = jnp.zeros(wbig.shape, BF16)
    for k in range(layers):
        for a in range(3):
            tap = a + core * (2 - 2 * a)
            for b in range(3):
                w = w_v[k, tap, b]
                for h in range(2):
                    wbig[k, (a + h) * chans : (a + h + 1) * chans,
                         (3 * h + b) * chans : (3 * h + b + 1) * chans] = w

    for u in range(lines + 1):
        if u < lines:
            @pl.when(has_l)
            def _():
                halo_copy(u).wait_recv()

            partial_lse(u, False)

            @pl.when(has_l)
            def _():
                mt_down(u).start()

        if u > 0:
            @pl.when(has_l)
            def _():
                c2_up(u - 1).wait_recv()

            @pl.when(has_r)
            def _():
                c2_down(u - 1).wait_recv()

            transport(u - 1)
            for cond, _, copy in line_copies(u - 1):
                @pl.when(cond)
                def _():
                    copy.start()

        if u < lines:
            @pl.when(has_l)
            def _():
                mt_up(u).wait_recv()

            @pl.when(has_r)
            def _():
                mt_down(u).wait_recv()

            row_pass(u)

            @pl.when(has_r)
            def _():
                c2_up(u).start()

            @pl.when(has_l)
            def _():
                c2_down(u).start()

    for _, cond, copy in line_copies(None):
        @pl.when(cond)
        def _():
            copy.wait_recv()

    part = wide // 3 if (wide // 3) % 16 == 0 else wide
    step_rows = 96

    def conv_pair(src, k, slot, store):
        for g in range(wide // part):
            rows = slice(g * part, (g + 1) * part)
            ins = jnp.concatenate([src[slot - 1 + i, rows, :] for i in range(4)], axis=1)
            y = jnp.dot(ins, wbig[k], preferred_element_type=F32)
            for j in range(6):
                y_ref[j, 8 + g * part : 8 + (g + 1) * part, :] = y[:, j * chans : (j + 1) * chans]
        for h in range(2):
            store(h, src, slot + h, bias_ref[k : k + 1, :])

    def updated(h, src, slot, bias, at, rows):
        total = (
            y_ref[3 * h, 7 + at : 7 + at + rows, :]
            + y_ref[3 * h + 1, 8 + at : 8 + at + rows, :]
            + y_ref[3 * h + 2, 9 + at : 9 + at + rows, :]
        )
        state = src[slot, at : at + rows, :].astype(F32)
        return (state + jnp.maximum(total + bias, 0.0)).astype(BF16)

    def layer(src, dst, k, first, last):
        def keep(h, src, slot, bias):
            for at in range(0, wide, step_rows):
                dst[slot, at : at + step_rows, :] = updated(h, src, slot, bias, at, step_rows)

        for slot in range(first, last, 2):
            conv_pair(src, k, slot, keep)

        @pl.when(jnp.logical_not(has_l))
        def _():
            dst[first:last, 0:PAD, :] = jnp.zeros((last - first, PAD, chans), BF16)

        @pl.when(jnp.logical_not(has_r))
        def _():
            dst[first:last, n + PAD : wide, :] = jnp.zeros((last - first, PAD, chans), BF16)

        @pl.when(jnp.logical_not(has_x))
        def _():
            dst[first:REACH] = jnp.zeros((REACH - first, wide, chans), BF16)

    layer(x0, x1, 0, 1, lines + 5)
    layer(x1, x2, 1, 2, lines + 4)

    def put(h, src, slot, bias):
        ln = line_of(slot - REACH)
        for at in range(0, n, 128):
            out_ref[ln, at : at + 128, :] = updated(h, src, slot, bias, at + PAD, 128)

    for slot in range(REACH, REACH + lines, 2):
        conv_pair(x2, 2, slot, put)

    @pl.when(has_r)
    def _():
        for u in range(lines):
            halo_copy(u).wait_send()
            mt_up(u).wait_send()
            c2_up(u).wait_send()

    @pl.when(has_l)
    def _():
        for u in range(lines):
            mt_down(u).wait_send()
            c2_down(u).wait_send()

    for cond, _, copy in line_copies(None):
        @pl.when(cond)
        def _():
            copy.wait_send()


def shards(segs, line_devs, left, right, weight, bias):
    lines, n, chans = left.shape
    layers = weight.shape[0]
    blk = n // 4
    wide = n + 2 * PAD
    slots = lines + 2 * REACH
    shape = (segs, line_devs, lines, n, blk, chans, layers)
    dma = pltpu.SemaphoreType.DMA
    vm = pltpu.VMEM
    return pl.pallas_call(
        functools.partial(body, shape),
        out_shape=(
            jax.ShapeDtypeStruct((lines, n, chans), BF16),
            jax.ShapeDtypeStruct((lines, n), F32),
        ),
        in_specs=[pl.BlockSpec(memory_space=pl.ANY)] * 3 + [pl.BlockSpec(memory_space=vm)],
        out_specs=(pl.BlockSpec(memory_space=vm), pl.BlockSpec(memory_space=vm)),
        scratch_shapes=[
            vm((lines, n, chans), BF16),
            vm((lines, 2 * n, chans), BF16),
            vm((2 * n, chans), BF16),
            vm((lines, 4, blk, n + blk), F32),
            vm((lines, 2, n), F32),
            vm((lines, 2, n), F32),
            vm((lines, 2, n), F32),
            vm((lines, 2, n), F32),
            vm((8, 2 * n), F32),
            vm((8, 2 * n), F32),
            vm((lines, 1, n), F32),
            vm((lines, 1, n), F32),
            vm((lines, 1, n), F32),
            vm((lines, 1, n), F32),
            vm(weight.shape, BF16),
            vm((layers, 4 * chans, 6 * chans), BF16),
            vm((slots, wide, chans), BF16),
            vm((slots, wide, chans), BF16),
            vm((slots, wide, chans), BF16),
            vm((6, wide + 16, chans), F32),
            dma((lines, 2)),
            dma,
            dma((lines,)),
            dma((lines,)),
            dma((lines, 2)),
            dma((lines, 2)),
            dma((lines, 2)),
            dma((lines, 2)),
            dma((lines, 3, 3)),
            dma((slots, 3)),
        ],
        compiler_params=pltpu.CompilerParams(
            collective_id=0, has_side_effects=True, vmem_limit_bytes=60 * 1024 * 1024
        ),
        name="stereo",
    )(left, right, weight, bias)


def solution(mesh):
    return jax.shard_map(
        functools.partial(shards, mesh.shape["seg"], mesh.shape["lines"]),
        mesh=mesh,
        in_specs=(P("lines", "seg", None), P("lines", "seg", None), P(), P()),
        out_specs=(P("lines", "seg", None), P("lines", "seg")),
        check_vma=False,
    )
```

```python
import functools
import math

import jax
import jax.numpy as jnp
from jax import lax
from jax.experimental import pallas as pl
from jax.experimental.pallas import tpu as pltpu
from jax.sharding import PartitionSpec as P

NEG = -1e30
LOG2E = 1.4426950408889634
PAD = 16
REACH = 3
MESH = pl.DeviceIdType.MESH
F32 = jnp.float32
BF16 = jnp.bfloat16


def nt_dot(a, b):
    return lax.dot_general(a, b, (((1,), (1,)), ((), ())), preferred_element_type=F32)


def groups(x):
    return x.reshape(x.shape[0] // 8, 8, x.shape[1])


def body(
    shape, left_hbm, right_hbm, w_hbm, bias_ref, out_ref, disp_ref,
    left_v, right_v, tcol, s_ref, rm_ref, iv_ref, own_mt, halo_mt, own_in, halo_in, c1, c2acc,
    own_c2, halo_c2, own_c2_in, halo_c2_in, w_v, wbig, x0, x1, x2, y_ref,
    load_sem, wsem, halo_ss, halo_rs, mt_ss, mt_rs, c2_ss, c2_rs, ln_ss, ln_rs,
):
    segs, line_devs, lines, n, blk, chans, layers = shape
    nblk = n // blk
    win = n + blk
    wide = n + 2 * PAD
    scale = LOG2E / math.sqrt(chans)
    seg = lax.axis_index("seg")
    me = lax.axis_index("lines")
    core = lax.rem(me, 2)
    mate = me + 1 - 2 * core
    cross = me - 1 + 2 * core
    has_l = seg > 0
    has_r = seg < segs - 1
    has_x = (cross >= 0) & (cross < line_devs)

    def dev(ds, ln):
        return {"seg": seg + ds, "lines": ln}

    def line_of(u):
        return u + core * (lines - 1 - 2 * u)

    def remote(src, dst, ss, rs, where):
        return pltpu.make_async_remote_copy(
            src_ref=src, dst_ref=dst, send_sem=ss, recv_sem=rs, device_id=where, device_id_type=MESH
        )

    barrier = pltpu.get_barrier_semaphore()
    peers = []
    for ds, side in ((-1, has_l), (1, has_r)):
        peers += [(side, dev(ds, me)), (side, dev(ds, mate)), (side & has_x, dev(ds, cross))]
    peers += [(me >= 0, dev(0, mate)), (has_x, dev(0, cross))]
    for cond, where in peers:
        @pl.when(cond)
        def _():
            pl.semaphore_signal(barrier, inc=1, device_id=where, device_id_type=MESH)

    def load(u, which):
        src = (left_hbm, right_hbm)[which].at[line_of(u)]
        dst = left_v.at[u] if which == 0 else right_v.at[u, pl.ds(n, n)]
        return pltpu.make_async_copy(src, dst, load_sem.at[u, which])

    for u in range(lines):
        load(u, 0).start()
        load(u, 1).start()
    wload = pltpu.make_async_copy(w_hbm, w_v, wsem)
    wload.start()

    pl.semaphore_wait(barrier, sum(cond.astype(jnp.int32) for cond, _ in peers))

    def halo_copy(u):
        return remote(
            right_hbm.at[line_of(u)], right_v.at[u, pl.ds(0, n)], halo_ss.at[u], halo_rs.at[u],
            dev(1, me),
        )

    def send_halo(u):
        @pl.when(has_r)
        def _():
            halo_copy(u).start()

    send_halo(0)

    def mt_up(u):
        return remote(own_mt.at[u], halo_in.at[u], mt_ss.at[u, 0], mt_rs.at[u, 0], dev(1, me))

    def mt_down(u):
        return remote(halo_mt.at[u], own_in.at[u], mt_ss.at[u, 1], mt_rs.at[u, 1], dev(-1, me))

    def c2_up(u):
        return remote(own_c2.at[u], halo_c2_in.at[u], c2_ss.at[u, 0], c2_rs.at[u, 0], dev(1, me))

    def c2_down(u):
        return remote(halo_c2.at[u], own_c2_in.at[u], c2_ss.at[u, 1], c2_rs.at[u, 1], dev(-1, me))

    def line_routes():
        routes = []
        for u in range(lines):
            routes.append((u, u + REACH, None, 0, me))
            if u < REACH:
                routes.append((u, REACH - 1 - u, has_x, 1, cross))
            if u >= lines - REACH:
                routes.append((u, 2 * lines + REACH - 1 - u, None, 2, mate))
        return routes

    def line_copies(u_pick, slots=None):
        copies = []
        for u, slot, cond, to, ln in line_routes():
            if u_pick is not None and u != u_pick or slots is not None and slot not in slots:
                continue
            mine = u + REACH
            cond = me >= 0 if cond is None else cond
            if to:
                copies.append((cond, cond, remote(
                    x0.at[mine, pl.ds(PAD, n)], x0.at[slot, pl.ds(PAD, n)],
                    ln_ss.at[u, to, 0], ln_rs.at[slot, 0], dev(0, ln))))
            copies.append((cond & has_r, cond & has_l, remote(
                x0.at[mine, pl.ds(n, PAD)], x0.at[slot, pl.ds(0, PAD)],
                ln_ss.at[u, to, 1], ln_rs.at[slot, 1], dev(1, ln))))
            copies.append((cond & has_l, cond & has_r, remote(
                x0.at[mine, pl.ds(PAD, PAD)], x0.at[slot, pl.ds(n + PAD, PAD)],
                ln_ss.at[u, to, 2], ln_rs.at[slot, 2], dev(-1, ln))))
        return copies

    e_ids = lax.broadcasted_iota(jnp.int32, (2 * n, chans), 0)
    lane = lax.broadcasted_iota(jnp.int32, (2 * n, chans), 1)
    t = n - e_ids
    low = t & 7
    tcol[...] = jnp.where(
        lane == 0, 1, jnp.where(lane == 1, t - low, jnp.where(lane == 2, low, 0))
    ).astype(F32).astype(BF16)

    @pl.when(jnp.logical_not(has_l))
    def _():
        right_v[:, 0:n, :] = jnp.zeros((lines, n, chans), BF16)
        halo_in[:, 0:1, :] = jnp.full((lines, 1, n), NEG, F32)
        halo_in[:, 1:2, :] = jnp.zeros((lines, 1, n), F32)
        halo_c2_in[...] = jnp.zeros((lines, 1, n), F32)
        x0[:, 0:PAD, :] = jnp.zeros((lines + 2 * REACH, PAD, chans), BF16)

    @pl.when(jnp.logical_not(has_r))
    def _():
        own_in[:, 0:1, :] = jnp.full((lines, 1, n), NEG, F32)
        own_in[:, 1:2, :] = jnp.zeros((lines, 1, n), F32)
        own_c2_in[...] = jnp.zeros((lines, 1, n), F32)
        x0[:, n + PAD : wide, :] = jnp.zeros((lines + 2 * REACH, PAD, chans), BF16)

    @pl.when(jnp.logical_not(has_x))
    def _():
        x0[0:REACH] = jnp.zeros((REACH, wide, chans), BF16)

    y_ref[:, 0:8, :] = jnp.zeros((6, 8, chans), F32)
    y_ref[:, 8 + wide : 16 + wide, :] = jnp.zeros((6, 8, chans), F32)

    il = lax.broadcasted_iota(jnp.int32, (blk, blk), 0)
    jl = lax.broadcasted_iota(jnp.int32, (blk, blk), 1)

    def partial_lse(u, own):
        base = n if own else 0
        dst = own_mt if own else halo_mt
        for c in range(nblk):
            cols = right_v[u, base + c * blk : base + (c + 1) * blk, :]
            run_m = jnp.full((8, blk), NEG, F32)
            run_t = jnp.zeros((8, blk), F32)
            for r in range(c, nblk) if own else range(c + 1):
                s = nt_dot(left_v[u, r * blk : (r + 1) * blk, :], cols) * scale
                if r == c:
                    s = jnp.where(jl <= il if own else jl > il, s, NEG)
                at = base + (c - r) * blk
                s_ref[u, r * blk : (r + 1) * blk, at : at + blk] = s
                g = groups(s)
                m = jnp.maximum(run_m, jnp.max(g, axis=0))
                run_t = run_t * jnp.exp2(run_m - m) + jnp.sum(jnp.exp2(g - m[None]), axis=0)
                run_m = m
            m = jnp.max(run_m, axis=0, keepdims=True)
            dst[u, 0:1, c * blk : (c + 1) * blk] = m
            dst[u, 1:2, c * blk : (c + 1) * blk] = jnp.sum(
                run_t * jnp.exp2(run_m - m), axis=0, keepdims=True
            )

    def col_pot(a, b):
        m = jnp.maximum(a[0:1], b[0:1])
        tot = a[1:2] * jnp.exp2(a[0:1] - m) + b[1:2] * jnp.exp2(b[0:1] - m)
        return -(m + jnp.log(tot) * LOG2E)

    rows_at = min(64, blk)
    steps = n // rows_at
    tiles = [slice(j * 128, min(win, (j + 1) * 128)) for j in range(-(-win // 128))]

    def pot_at(k):
        return pl.multiple_of((k * rows_at) // blk * blk, blk)

    def row_max(u, k):
        here = pl.ds(pl.multiple_of(k * rows_at, rows_at), rows_at)
        top = None
        for tile in tiles:
            width = tile.stop - tile.start
            pot = c1[:, pl.ds(pot_at(k) + tile.start, width)]
            t = groups(s_ref[u, here, tile]) + pot[None]
            s_ref[u, here, tile] = t.reshape(rows_at, width)
            if width < 128:
                t = jnp.concatenate([t] * (128 // width), axis=2)
            top = t if top is None else jnp.maximum(top, t)
        top = jnp.max(top, axis=2, keepdims=True)
        rm_ref[here, :] = jnp.broadcast_to(top, (rows_at // 8, 8, chans)).reshape(rows_at, chans)

    def row_exp(u, k):
        here = pl.ds(pl.multiple_of(k * rows_at, rows_at), rows_at)
        top = groups(rm_ref[here, :])
        total = jnp.zeros((rows_at // 8, 8, 1), F32)
        acc = None
        for tile in tiles:
            width = tile.stop - tile.start
            e = jnp.exp2(groups(s_ref[u, here, tile]) - top[:, :, :width])
            s_ref[u, here, tile] = e.reshape(rows_at, width)
            if width < 128:
                total = total + jnp.sum(e, axis=2, keepdims=True)
            else:
                acc = e if acc is None else acc + e
        inv = 1.0 / (total + jnp.sum(acc, axis=2, keepdims=True))
        iv_ref[here, :] = jnp.broadcast_to(inv, (rows_at // 8, 8, chans)).reshape(rows_at, chans)

    def col_sum(u, k):
        here = pl.ds(pl.multiple_of(k * rows_at, rows_at), rows_at)
        inv = groups(iv_ref[here, :])
        for tile in tiles:
            width = tile.stop - tile.start
            part = jnp.sum(groups(s_ref[u, here, tile]) * inv[:, :, :width], axis=0)
            c2acc[:, pl.ds(pot_at(k) + tile.start, width)] += part

    def row_pass(u):
        own = col_pot(own_mt[u], own_in[u])
        halo = jnp.where(has_l, col_pot(halo_mt[u], halo_in[u]), NEG)
        c1[:, n : 2 * n] = jnp.broadcast_to(own, (8, n))
        c1[:, 0:n] = jnp.broadcast_to(halo, (8, n))
        c2acc[...] = jnp.zeros((8, 2 * n), F32)
        row_max(u, 0)
        row_exp(u, 0)
        row_max(u, 1)

        def step(k, carry):
            col_sum(u, k - 2)
            row_max(u, k)
            row_exp(u, k - 1)
            return carry

        lax.fori_loop(2, steps, step, 0)
        col_sum(u, steps - 2)
        row_exp(u, steps - 1)
        col_sum(u, steps - 1)
        halo_c2[u] = jnp.sum(c2acc[:, 0:n], axis=0, keepdims=True)
        own_c2[u] = jnp.sum(c2acc[:, n : 2 * n], axis=0, keepdims=True)

    def transport(u):
        c1[:, n : 2 * n] = jnp.broadcast_to(1.0 / (own_c2[u] + own_c2_in[u]), (8, n))
        c1[:, 0:n] = jnp.broadcast_to(
            jnp.where(has_l, 1.0 / (halo_c2[u] + halo_c2_in[u]), 0.0), (8, n)
        )
        ln = line_of(u)

        def step(r, carry):
            at = pl.multiple_of(r * blk, blk)
            q = groups(s_ref[u, pl.ds(at, blk), :]) * c1[:, pl.ds(at, win)][None]
            q = q.reshape(blk, win).astype(BF16)
            rhs = jnp.concatenate([right_v[u, pl.ds(at, win), :], tcol[pl.ds(at, win), :]], axis=1)
            o = jnp.dot(q, rhs, preferred_element_type=F32)
            matched = o[:, :chans] / o[:, chans : chans + 1]
            x0[u + REACH, pl.ds(PAD + at, blk), :] = (
                matched - left_v[u, pl.ds(at, blk), :].astype(F32)
            ).astype(BF16)
            rowed = jnp.transpose(o[:, chans:])
            ids = (lax.broadcasted_iota(jnp.int32, (1, blk), 1) + at).astype(F32)
            disp_ref[pl.ds(ln, 1), pl.ds(at, blk)] = ids + (rowed[1:2] + rowed[2:3]) / rowed[0:1]
            return carry

        lax.fori_loop(0, nblk, step, 0)

    def own_step(u, carry):
        load(u, 0).wait()
        load(u, 1).wait()
        partial_lse(u, True)

        @pl.when(has_r)
        def _():
            mt_up(u).start()

        return carry

    lax.fori_loop(0, lines, own_step, 0)
    send_halo(1)

    wload.wait()
    wbig[...] = jnp.zeros(wbig.shape, BF16)
    for k in range(layers):
        for a in range(3):
            tap = a + core * (2 - 2 * a)
            for b in range(3):
                w = w_v[k, tap, b]
                for h in range(2):
                    wbig[k, (a + h) * chans : (a + h + 1) * chans,
                         (3 * h + b) * chans : (3 * h + b + 1) * chans] = w

    def scores_step(u):
        @pl.when(has_l)
        def _():
            halo_copy(u).wait_recv()

        partial_lse(u, False)

        @pl.when(has_l)
        def _():
            mt_down(u).start()

    def row_step(u):
        @pl.when(has_l)
        def _():
            mt_up(u).wait_recv()

        @pl.when(has_r)
        def _():
            mt_down(u).wait_recv()

        row_pass(u)

        @pl.when(has_r)
        def _():
            c2_up(u).start()

        @pl.when(has_l)
        def _():
            c2_down(u).start()

    def plan_step(u):
        @pl.when(has_l)
        def _():
            c2_up(u).wait_recv()

        @pl.when(has_r)
        def _():
            c2_down(u).wait_recv()

        transport(u)
        for cond, _, copy in line_copies(u):
            @pl.when(cond)
            def _():
                copy.start()

    def wait_slots(slots):
        for _, cond, copy in line_copies(None, slots):
            @pl.when(cond)
            def _():
                copy.wait_recv()

    part = wide // 3 if (wide // 3) % 16 == 0 else wide
    step_rows = 96

    def conv_pair(src, k, slot, store):
        for g in range(wide // part):
            rows = slice(g * part, (g + 1) * part)
            ins = jnp.concatenate([src[slot - 1 + i, rows, :] for i in range(4)], axis=1)
            y = jnp.dot(ins, wbig[k], preferred_element_type=F32)
            for j in range(6):
                y_ref[j, 8 + g * part : 8 + (g + 1) * part, :] = y[:, j * chans : (j + 1) * chans]
        for h in range(2):
            store(h, src, slot + h, bias_ref[k : k + 1, :])

    def updated(h, src, slot, bias, at, rows):
        total = (
            y_ref[3 * h, 7 + at : 7 + at + rows, :]
            + y_ref[3 * h + 1, 8 + at : 8 + at + rows, :]
            + y_ref[3 * h + 2, 9 + at : 9 + at + rows, :]
        )
        state = src[slot, at : at + rows, :].astype(F32)
        return (state + jnp.maximum(total + bias, 0.0)).astype(BF16)

    def clear_edges(dst, first, last):
        @pl.when(jnp.logical_not(has_l))
        def _():
            dst[first:last, 0:PAD, :] = jnp.zeros((last - first, PAD, chans), BF16)

        @pl.when(jnp.logical_not(has_r))
        def _():
            dst[first:last, n + PAD : wide, :] = jnp.zeros((last - first, PAD, chans), BF16)

        if first < REACH:
            stop = min(last, REACH)

            @pl.when(jnp.logical_not(has_x))
            def _():
                dst[first:stop] = jnp.zeros((stop - first, wide, chans), BF16)

    def layer_pair(src, dst, k, first):
        def keep(h, src, slot, bias):
            for at in range(0, wide, step_rows):
                dst[slot, at : at + step_rows, :] = updated(h, src, slot, bias, at, step_rows)

        conv_pair(src, k, first, keep)
        clear_edges(dst, first, first + 2)

    def put(h, src, slot, bias):
        ln = line_of(slot - REACH)
        for at in range(0, n, 128):
            out_ref[ln, at : at + 128, :] = updated(h, src, slot, bias, at + PAD, 128)

    for u in range(lines):
        scores_step(u)
        if u >= 1:
            row_step(u - 1)
        if u + 2 < lines:
            send_halo(u + 2)
        if u >= 2:
            plan_step(u - 2)
    row_step(lines - 1)
    plan_step(lines - 2)
    wait_slots((2, 3, 4, 5))
    layer_pair(x0, x1, 0, 3)
    plan_step(lines - 1)
    wait_slots((0, 1))
    layer_pair(x0, x1, 0, 1)
    layer_pair(x1, x2, 1, 2)
    wait_slots((6, 7, 8, 9))
    layer_pair(x0, x1, 0, 5)
    layer_pair(x0, x1, 0, 7)
    layer_pair(x1, x2, 1, 4)
    layer_pair(x1, x2, 1, 6)
    conv_pair(x2, 2, 3, put)
    conv_pair(x2, 2, 5, put)

    @pl.when(has_r)
    def _():
        for u in range(lines):
            halo_copy(u).wait_send()
            mt_up(u).wait_send()
            c2_up(u).wait_send()

    @pl.when(has_l)
    def _():
        for u in range(lines):
            mt_down(u).wait_send()
            c2_down(u).wait_send()

    for cond, _, copy in line_copies(None):
        @pl.when(cond)
        def _():
            copy.wait_send()


def shards(segs, line_devs, left, right, weight, bias):
    lines, n, chans = left.shape
    layers = weight.shape[0]
    blk = n // 4
    wide = n + 2 * PAD
    slots = lines + 2 * REACH
    shape = (segs, line_devs, lines, n, blk, chans, layers)
    dma = pltpu.SemaphoreType.DMA
    vm = pltpu.VMEM
    return pl.pallas_call(
        functools.partial(body, shape),
        out_shape=(
            jax.ShapeDtypeStruct((lines, n, chans), BF16),
            jax.ShapeDtypeStruct((lines, n), F32),
        ),
        in_specs=[pl.BlockSpec(memory_space=pl.ANY)] * 3 + [pl.BlockSpec(memory_space=vm)],
        out_specs=(pl.BlockSpec(memory_space=vm), pl.BlockSpec(memory_space=vm)),
        scratch_shapes=[
            vm((lines, n, chans), BF16),
            vm((lines, 2 * n, chans), BF16),
            vm((2 * n, chans), BF16),
            vm((lines, n, n + blk), F32),
            vm((n, chans), F32),
            vm((n, chans), F32),
            vm((lines, 2, n), F32),
            vm((lines, 2, n), F32),
            vm((lines, 2, n), F32),
            vm((lines, 2, n), F32),
            vm((8, 2 * n), F32),
            vm((8, 2 * n), F32),
            vm((lines, 1, n), F32),
            vm((lines, 1, n), F32),
            vm((lines, 1, n), F32),
            vm((lines, 1, n), F32),
            vm(weight.shape, BF16),
            vm((layers, 4 * chans, 6 * chans), BF16),
            vm((slots, wide, chans), BF16),
            vm((slots, wide, chans), BF16),
            vm((slots, wide, chans), BF16),
            vm((6, wide + 16, chans), F32),
            dma((lines, 2)),
            dma,
            dma((lines,)),
            dma((lines,)),
            dma((lines, 2)),
            dma((lines, 2)),
            dma((lines, 2)),
            dma((lines, 2)),
            dma((lines, 3, 3)),
            dma((slots, 3)),
        ],
        compiler_params=pltpu.CompilerParams(
            collective_id=0, has_side_effects=True, vmem_limit_bytes=60 * 1024 * 1024
        ),
        name="stereo",
    )(left, right, weight, bias)


def solution(mesh):
    return jax.shard_map(
        functools.partial(shards, mesh.shape["seg"], mesh.shape["lines"]),
        mesh=mesh,
        in_specs=(P("lines", "seg", None), P("lines", "seg", None), P(), P()),
        out_specs=(P("lines", "seg", None), P("lines", "seg")),
        check_vma=False,
    )
```

```python
import functools
import math

import jax
import jax.numpy as jnp
from jax import lax
from jax.experimental import pallas as pl
from jax.experimental.pallas import tpu as pltpu
from jax.sharding import PartitionSpec as P

NEG = -1e30
LOG2E = 1.4426950408889634
PAD = 16
REACH = 3
MESH = pl.DeviceIdType.MESH
F32 = jnp.float32
BF16 = jnp.bfloat16


def nt_dot(a, b):
    return lax.dot_general(a, b, (((1,), (1,)), ((), ())), preferred_element_type=F32)


def groups(x):
    return x.reshape(x.shape[0] // 8, 8, x.shape[1])


def body(
    shape, left_hbm, right_hbm, w_hbm, bias_ref, out_ref, disp_ref,
    left_v, right_v, tcol, s_ref, k_ref, own_mt, halo_mt, own_in, halo_in, c1, c2acc,
    own_c2, halo_c2, own_c2_in, halo_c2_in, w_v, wbig, x0, x1, x2, y_ref,
    load_sem, wsem, halo_ss, halo_rs, mt_ss, mt_rs, c2_ss, c2_rs, ln_ss, ln_rs,
):
    segs, line_devs, lines, n, blk, chans, layers = shape
    nblk = n // blk
    win = n + blk
    wide = n + 2 * PAD
    scale = LOG2E / math.sqrt(chans)
    seg = lax.axis_index("seg")
    me = lax.axis_index("lines")
    core = lax.rem(me, 2)
    mate = me + 1 - 2 * core
    cross = me - 1 + 2 * core
    has_l = seg > 0
    has_r = seg < segs - 1
    has_x = (cross >= 0) & (cross < line_devs)

    def dev(ds, ln):
        return {"seg": seg + ds, "lines": ln}

    def line_of(u):
        return u + core * (lines - 1 - 2 * u)

    def remote(src, dst, ss, rs, where):
        return pltpu.make_async_remote_copy(
            src_ref=src, dst_ref=dst, send_sem=ss, recv_sem=rs, device_id=where, device_id_type=MESH
        )

    barrier = pltpu.get_barrier_semaphore()
    peers = []
    for ds, side in ((-1, has_l), (1, has_r)):
        peers += [(side, dev(ds, me)), (side, dev(ds, mate)), (side & has_x, dev(ds, cross))]
    peers += [(me >= 0, dev(0, mate)), (has_x, dev(0, cross))]
    for cond, where in peers:
        @pl.when(cond)
        def _():
            pl.semaphore_signal(barrier, inc=1, device_id=where, device_id_type=MESH)

    def load(u, which):
        src = (left_hbm, right_hbm)[which].at[line_of(u)]
        dst = left_v.at[u] if which == 0 else right_v.at[u, pl.ds(n, n)]
        return pltpu.make_async_copy(src, dst, load_sem.at[u, which])

    for u in range(lines):
        load(u, 0).start()
        load(u, 1).start()
    wload = pltpu.make_async_copy(w_hbm, w_v, wsem)
    wload.start()

    pl.semaphore_wait(barrier, sum(cond.astype(jnp.int32) for cond, _ in peers))

    def halo_copy(u):
        return remote(
            right_hbm.at[line_of(u)], right_v.at[u, pl.ds(0, n)], halo_ss.at[u], halo_rs.at[u],
            dev(1, me),
        )

    def send_halo(u):
        @pl.when(has_r)
        def _():
            halo_copy(u).start()

    send_halo(0)

    def mt_up(u):
        return remote(own_mt.at[u], halo_in.at[u], mt_ss.at[u, 0], mt_rs.at[u, 0], dev(1, me))

    def mt_down(u):
        return remote(halo_mt.at[u], own_in.at[u], mt_ss.at[u, 1], mt_rs.at[u, 1], dev(-1, me))

    def c2_up(u):
        return remote(own_c2.at[u], halo_c2_in.at[u], c2_ss.at[u, 0], c2_rs.at[u, 0], dev(1, me))

    def c2_down(u):
        return remote(halo_c2.at[u], own_c2_in.at[u], c2_ss.at[u, 1], c2_rs.at[u, 1], dev(-1, me))

    def line_routes():
        routes = []
        for u in range(lines):
            routes.append((u, u + REACH, None, 0, me))
            if u < REACH:
                routes.append((u, REACH - 1 - u, has_x, 1, cross))
            if u >= lines - REACH:
                routes.append((u, 2 * lines + REACH - 1 - u, None, 2, mate))
        return routes

    def line_copies(u_pick, slots=None):
        copies = []
        for u, slot, cond, to, ln in line_routes():
            if u_pick is not None and u != u_pick or slots is not None and slot not in slots:
                continue
            mine = u + REACH
            cond = me >= 0 if cond is None else cond
            if to:
                copies.append((cond, cond, remote(
                    x0.at[mine, pl.ds(PAD, n)], x0.at[slot, pl.ds(PAD, n)],
                    ln_ss.at[u, to, 0], ln_rs.at[slot, 0], dev(0, ln))))
            copies.append((cond & has_r, cond & has_l, remote(
                x0.at[mine, pl.ds(n, PAD)], x0.at[slot, pl.ds(0, PAD)],
                ln_ss.at[u, to, 1], ln_rs.at[slot, 1], dev(1, ln))))
            copies.append((cond & has_l, cond & has_r, remote(
                x0.at[mine, pl.ds(PAD, PAD)], x0.at[slot, pl.ds(n + PAD, PAD)],
                ln_ss.at[u, to, 2], ln_rs.at[slot, 2], dev(-1, ln))))
        return copies

    e_ids = lax.broadcasted_iota(jnp.int32, (2 * n, chans), 0)
    lane = lax.broadcasted_iota(jnp.int32, (2 * n, chans), 1)
    t = n - e_ids
    low = t & 7
    tcol[...] = jnp.where(
        lane == 0, 1, jnp.where(lane == 1, t - low, jnp.where(lane == 2, low, 0))
    ).astype(F32).astype(BF16)

    @pl.when(jnp.logical_not(has_l))
    def _():
        right_v[:, 0:n, :] = jnp.zeros((lines, n, chans), BF16)
        halo_in[:, 0:1, :] = jnp.full((lines, 1, n), NEG, F32)
        halo_in[:, 1:2, :] = jnp.zeros((lines, 1, n), F32)
        halo_c2_in[...] = jnp.zeros((lines, 1, n), F32)
        x0[:, 0:PAD, :] = jnp.zeros((lines + 2 * REACH, PAD, chans), BF16)

    @pl.when(jnp.logical_not(has_r))
    def _():
        own_in[:, 0:1, :] = jnp.full((lines, 1, n), NEG, F32)
        own_in[:, 1:2, :] = jnp.zeros((lines, 1, n), F32)
        own_c2_in[...] = jnp.zeros((lines, 1, n), F32)
        x0[:, n + PAD : wide, :] = jnp.zeros((lines + 2 * REACH, PAD, chans), BF16)

    @pl.when(jnp.logical_not(has_x))
    def _():
        x0[0:REACH] = jnp.zeros((REACH, wide, chans), BF16)

    y_ref[:, 0:8, :] = jnp.zeros((6, 8, chans), F32)
    y_ref[:, 8 + wide : 16 + wide, :] = jnp.zeros((6, 8, chans), F32)

    il = lax.broadcasted_iota(jnp.int32, (blk // 2, blk), 0)
    jl = lax.broadcasted_iota(jnp.int32, (blk // 2, blk), 1)

    def partial_lse(u, own):
        base = n if own else 0
        dst = own_mt if own else halo_mt
        for c in range(nblk):
            cols = right_v[u, base + c * blk : base + (c + 1) * blk, :]
            pieces = []
            top = jnp.full((8, blk), NEG, F32)
            for r in range(c, nblk) if own else range(c + 1):
                at = base + (c - r) * blk
                for h in range(2):
                    rows = slice(r * blk + h * (blk // 2), r * blk + (h + 1) * (blk // 2))
                    s = nt_dot(left_v[u, rows, :], cols) * scale
                    if r == c:
                        ih = il + h * (blk // 2)
                        s = jnp.where(jl <= ih if own else jl > ih, s, NEG)
                    s_ref[u, rows, at : at + blk] = s
                    top = jnp.maximum(top, jnp.max(groups(s), axis=0))
                    pieces.append((rows, at))
            total = jnp.zeros((8, blk), F32)
            for rows, at in pieces:
                g = groups(s_ref[u, rows, at : at + blk])
                total = total + jnp.sum(jnp.exp2(g - top[None]), axis=0)
            m = jnp.max(top, axis=0, keepdims=True)
            dst[u, 0:1, c * blk : (c + 1) * blk] = m
            dst[u, 1:2, c * blk : (c + 1) * blk] = jnp.sum(
                total * jnp.exp2(top - m), axis=0, keepdims=True
            )

    def col_pot(a, b):
        m = jnp.maximum(a[0:1], b[0:1])
        tot = a[1:2] * jnp.exp2(a[0:1] - m) + b[1:2] * jnp.exp2(b[0:1] - m)
        return -(m + jnp.log(tot) * LOG2E)

    rows_at = min(64, blk)
    steps = n // rows_at
    tiles = [slice(j * 128, min(win, (j + 1) * 128)) for j in range(-(-win // 128))]

    def pot_at(k):
        return pl.multiple_of((k * rows_at) // blk * blk, blk)

    def row_max(u, k):
        here = pl.ds(pl.multiple_of(k * rows_at, rows_at), rows_at)
        top = None
        for tile in tiles:
            width = tile.stop - tile.start
            pot = c1[:, pl.ds(pot_at(k) + tile.start, width)]
            t = groups(s_ref[u, here, tile]) + pot[None]
            if width < 128:
                t = jnp.concatenate([t] * (128 // width), axis=2)
            top = t if top is None else jnp.maximum(top, t)
        return jnp.broadcast_to(jnp.max(top, axis=2, keepdims=True), top.shape)

    def row_exp(u, k, top):
        here = pl.ds(pl.multiple_of(k * rows_at, rows_at), rows_at)
        total = None
        for tile in tiles:
            width = tile.stop - tile.start
            pot = c1[:, pl.ds(pot_at(k) + tile.start, width)]
            t = groups(s_ref[u, here, tile]) + pot[None]
            e = jnp.exp2(t - top[:, :, :width])
            k_ref[u % 2, here, tile] = e.reshape(rows_at, width)
            if width < 128:
                e = jnp.concatenate([e, jnp.zeros(e.shape[:2] + (128 - width,), F32)], axis=2)
            total = e if total is None else total + e
        return jnp.broadcast_to(1.0 / jnp.sum(total, axis=2, keepdims=True), total.shape)

    def col_sum(u, k, inv):
        here = pl.ds(pl.multiple_of(k * rows_at, rows_at), rows_at)
        for tile in tiles:
            width = tile.stop - tile.start
            part = jnp.sum(groups(k_ref[u % 2, here, tile]) * inv[:, :, :width], axis=0)
            c2acc[:, pl.ds(pot_at(k) + tile.start, width)] += part

    def row_pass(u):
        own = col_pot(own_mt[u], own_in[u])
        halo = jnp.where(has_l, col_pot(halo_mt[u], halo_in[u]), NEG)
        c1[:, n : 2 * n] = jnp.broadcast_to(own, (8, n))
        c1[:, 0:n] = jnp.broadcast_to(halo, (8, n))
        c2acc[...] = jnp.zeros((8, 2 * n), F32)
        inv = row_exp(u, 0, row_max(u, 0))
        top = row_max(u, 1)

        def step(k, carry):
            top, inv = carry
            col_sum(u, k - 2, inv)
            inv = row_exp(u, k - 1, top)
            return row_max(u, k), inv

        top, inv = lax.fori_loop(2, steps, step, (top, inv))
        col_sum(u, steps - 2, inv)
        col_sum(u, steps - 1, row_exp(u, steps - 1, top))
        halo_c2[u] = jnp.sum(c2acc[:, 0:n], axis=0, keepdims=True)
        own_c2[u] = jnp.sum(c2acc[:, n : 2 * n], axis=0, keepdims=True)

    def transport(u):
        c1[:, n : 2 * n] = jnp.broadcast_to(1.0 / (own_c2[u] + own_c2_in[u]), (8, n))
        c1[:, 0:n] = jnp.broadcast_to(
            jnp.where(has_l, 1.0 / (halo_c2[u] + halo_c2_in[u]), 0.0), (8, n)
        )
        ln = line_of(u)

        for at in range(0, n, blk):
            q = groups(k_ref[u % 2, pl.ds(at, blk), :]) * c1[:, pl.ds(at, win)][None]
            q = q.reshape(blk, win).astype(BF16)
            rhs = jnp.concatenate([right_v[u, pl.ds(at, win), :], tcol[pl.ds(at, win), :]], axis=1)
            o = jnp.dot(q, rhs, preferred_element_type=F32)
            matched = o[:, :chans] * (1.0 / o[:, chans : chans + 1])
            x0[u + REACH, pl.ds(PAD + at, blk), :] = (
                matched - left_v[u, pl.ds(at, blk), :].astype(F32)
            ).astype(BF16)
            rowed = jnp.transpose(o[:, chans:])
            ids = (lax.broadcasted_iota(jnp.int32, (1, blk), 1) + at).astype(F32)
            disp_ref[pl.ds(ln, 1), pl.ds(at, blk)] = ids + (rowed[1:2] + rowed[2:3]) / rowed[0:1]

    def own_step(u, carry):
        load(u, 0).wait()
        load(u, 1).wait()
        partial_lse(u, True)

        @pl.when(has_r)
        def _():
            mt_up(u).start()

        return carry

    lax.fori_loop(0, lines, own_step, 0)
    send_halo(1)

    wload.wait()
    wbig[...] = jnp.zeros(wbig.shape, BF16)
    for k in range(layers):
        for a in range(3):
            tap = a + core * (2 - 2 * a)
            for b in range(3):
                w = w_v[k, tap, b]
                for h in range(2):
                    wbig[k, (a + h) * chans : (a + h + 1) * chans,
                         (3 * h + b) * chans : (3 * h + b + 1) * chans] = w

    def scores_step(u):
        @pl.when(has_l)
        def _():
            halo_copy(u).wait_recv()

        partial_lse(u, False)

        @pl.when(has_l)
        def _():
            mt_down(u).start()

    def row_step(u):
        @pl.when(has_l)
        def _():
            mt_up(u).wait_recv()

        @pl.when(has_r)
        def _():
            mt_down(u).wait_recv()

        row_pass(u)

        @pl.when(has_r)
        def _():
            c2_up(u).start()

        @pl.when(has_l)
        def _():
            c2_down(u).start()

    def plan_step(u):
        @pl.when(has_l)
        def _():
            c2_up(u).wait_recv()

        @pl.when(has_r)
        def _():
            c2_down(u).wait_recv()

        transport(u)
        for cond, _, copy in line_copies(u):
            @pl.when(cond)
            def _():
                copy.start()

    def wait_slots(slots):
        for _, cond, copy in line_copies(None, slots):
            @pl.when(cond)
            def _():
                copy.wait_recv()

    part = wide // 3 if (wide // 3) % 16 == 0 else wide
    step_rows = 96

    def conv_pair(src, k, slot, store):
        for g in range(wide // part):
            rows = slice(g * part, (g + 1) * part)
            ins = jnp.concatenate([src[slot - 1 + i, rows, :] for i in range(4)], axis=1)
            y = jnp.dot(ins, wbig[k], preferred_element_type=F32)
            for j in range(6):
                y_ref[j, 8 + g * part : 8 + (g + 1) * part, :] = y[:, j * chans : (j + 1) * chans]
        for h in range(2):
            store(h, src, slot + h, bias_ref[k : k + 1, :])

    def updated(h, src, slot, bias, at, rows):
        total = (
            y_ref[3 * h, 7 + at : 7 + at + rows, :]
            + y_ref[3 * h + 1, 8 + at : 8 + at + rows, :]
            + y_ref[3 * h + 2, 9 + at : 9 + at + rows, :]
        )
        state = src[slot, at : at + rows, :].astype(F32)
        return (state + jnp.maximum(total + bias, 0.0)).astype(BF16)

    def clear_edges(dst, first, last):
        @pl.when(jnp.logical_not(has_l))
        def _():
            dst[first:last, 0:PAD, :] = jnp.zeros((last - first, PAD, chans), BF16)

        @pl.when(jnp.logical_not(has_r))
        def _():
            dst[first:last, n + PAD : wide, :] = jnp.zeros((last - first, PAD, chans), BF16)

        if first < REACH:
            stop = min(last, REACH)

            @pl.when(jnp.logical_not(has_x))
            def _():
                dst[first:stop] = jnp.zeros((stop - first, wide, chans), BF16)

    def layer_pair(src, dst, k, first):
        def keep(h, src, slot, bias):
            for at in range(0, wide, step_rows):
                dst[slot, at : at + step_rows, :] = updated(h, src, slot, bias, at, step_rows)

        conv_pair(src, k, first, keep)
        clear_edges(dst, first, first + 2)

    def put(h, src, slot, bias):
        ln = line_of(slot - REACH)
        for at in range(0, n, 128):
            out_ref[ln, at : at + 128, :] = updated(h, src, slot, bias, at + PAD, 128)

    for u in range(lines):
        scores_step(u)
        if u >= 1:
            row_step(u - 1)
        if u + 2 < lines:
            send_halo(u + 2)
        if u >= 2:
            plan_step(u - 2)
    row_step(lines - 1)
    plan_step(lines - 2)
    wait_slots((2, 3, 4, 5))
    layer_pair(x0, x1, 0, 3)
    plan_step(lines - 1)
    wait_slots((0, 1))
    layer_pair(x0, x1, 0, 1)
    layer_pair(x1, x2, 1, 2)
    wait_slots((6, 7, 8, 9))
    layer_pair(x0, x1, 0, 5)
    layer_pair(x0, x1, 0, 7)
    layer_pair(x1, x2, 1, 4)
    layer_pair(x1, x2, 1, 6)
    conv_pair(x2, 2, 3, put)
    conv_pair(x2, 2, 5, put)

    @pl.when(has_r)
    def _():
        for u in range(lines):
            halo_copy(u).wait_send()
            mt_up(u).wait_send()
            c2_up(u).wait_send()

    @pl.when(has_l)
    def _():
        for u in range(lines):
            mt_down(u).wait_send()
            c2_down(u).wait_send()

    for cond, _, copy in line_copies(None):
        @pl.when(cond)
        def _():
            copy.wait_send()


def shards(segs, line_devs, left, right, weight, bias):
    lines, n, chans = left.shape
    layers = weight.shape[0]
    blk = n // 4
    wide = n + 2 * PAD
    slots = lines + 2 * REACH
    shape = (segs, line_devs, lines, n, blk, chans, layers)
    dma = pltpu.SemaphoreType.DMA
    vm = pltpu.VMEM
    return pl.pallas_call(
        functools.partial(body, shape),
        out_shape=(
            jax.ShapeDtypeStruct((lines, n, chans), BF16),
            jax.ShapeDtypeStruct((lines, n), F32),
        ),
        in_specs=[pl.BlockSpec(memory_space=pl.ANY)] * 3 + [pl.BlockSpec(memory_space=vm)],
        out_specs=(pl.BlockSpec(memory_space=vm), pl.BlockSpec(memory_space=vm)),
        scratch_shapes=[
            vm((lines, n, chans), BF16),
            vm((lines, 2 * n, chans), BF16),
            vm((2 * n, chans), BF16),
            vm((lines, n, n + blk), F32),
            vm((2, n, n + blk), F32),
            vm((lines, 2, n), F32),
            vm((lines, 2, n), F32),
            vm((lines, 2, n), F32),
            vm((lines, 2, n), F32),
            vm((8, 2 * n), F32),
            vm((8, 2 * n), F32),
            vm((lines, 1, n), F32),
            vm((lines, 1, n), F32),
            vm((lines, 1, n), F32),
            vm((lines, 1, n), F32),
            vm(weight.shape, BF16),
            vm((layers, 4 * chans, 6 * chans), BF16),
            vm((slots, wide, chans), BF16),
            vm((slots, wide, chans), BF16),
            vm((slots, wide, chans), BF16),
            vm((6, wide + 16, chans), F32),
            dma((lines, 2)),
            dma,
            dma((lines,)),
            dma((lines,)),
            dma((lines, 2)),
            dma((lines, 2)),
            dma((lines, 2)),
            dma((lines, 2)),
            dma((lines, 3, 3)),
            dma((slots, 3)),
        ],
        compiler_params=pltpu.CompilerParams(
            collective_id=0, has_side_effects=True, vmem_limit_bytes=60 * 1024 * 1024
        ),
        name="stereo",
    )(left, right, weight, bias)


def solution(mesh):
    return jax.shard_map(
        functools.partial(shards, mesh.shape["seg"], mesh.shape["lines"]),
        mesh=mesh,
        in_specs=(P("lines", "seg", None), P("lines", "seg", None), P(), P()),
        out_specs=(P("lines", "seg", None), P("lines", "seg")),
        check_vma=False,
    )
```

```python
import functools
import math

import jax
import jax.numpy as jnp
from jax import lax
from jax.experimental import pallas as pl
from jax.experimental.pallas import tpu as pltpu
from jax.sharding import PartitionSpec as P

NEG = -1e30
LOG2E = 1.4426950408889634
PAD = 16
REACH = 3
MESH = pl.DeviceIdType.MESH
F32 = jnp.float32
BF16 = jnp.bfloat16


def nt_dot(a, b):
    return lax.dot_general(a, b, (((1,), (1,)), ((), ())), preferred_element_type=F32)


def groups(x):
    return x.reshape(x.shape[0] // 8, 8, x.shape[1])


def body(
    shape, left_hbm, right_hbm, w_hbm, bias_ref, out_ref, disp_ref,
    left_v, right_v, tcol, s_ref, k_ref, own_mt, halo_mt, own_in, halo_in, c1, c2acc,
    own_c2, halo_c2, own_c2_in, halo_c2_in, w_v, wbig, x0, x1, x2, y_ref,
    load_sem, wsem, halo_ss, halo_rs, mt_ss, mt_rs, c2_ss, c2_rs, ln_ss, ln_rs,
):
    segs, line_devs, lines, n, blk, chans, layers = shape
    nblk = n // blk
    win = n + blk
    wide = n + 2 * PAD
    scale = LOG2E / math.sqrt(chans)
    seg = lax.axis_index("seg")
    me = lax.axis_index("lines")
    core = lax.rem(me, 2)
    mate = me + 1 - 2 * core
    cross = me - 1 + 2 * core
    has_l = seg > 0
    has_r = seg < segs - 1
    has_x = (cross >= 0) & (cross < line_devs)

    def dev(ds, ln):
        return {"seg": seg + ds, "lines": ln}

    def line_of(u):
        return u + core * (lines - 1 - 2 * u)

    def remote(src, dst, ss, rs, where):
        return pltpu.make_async_remote_copy(
            src_ref=src, dst_ref=dst, send_sem=ss, recv_sem=rs, device_id=where, device_id_type=MESH
        )

    barrier = pltpu.get_barrier_semaphore()
    peers = []
    for ds, side in ((-1, has_l), (1, has_r)):
        peers += [(side, dev(ds, me)), (side, dev(ds, mate)), (side & has_x, dev(ds, cross))]
    peers += [(me >= 0, dev(0, mate)), (has_x, dev(0, cross))]
    for cond, where in peers:
        @pl.when(cond)
        def _():
            pl.semaphore_signal(barrier, inc=1, device_id=where, device_id_type=MESH)

    def load(u, which):
        src = (left_hbm, right_hbm)[which].at[line_of(u)]
        dst = left_v.at[u] if which == 0 else right_v.at[u, pl.ds(n, n)]
        return pltpu.make_async_copy(src, dst, load_sem.at[u, which])

    for u in range(lines):
        load(u, 0).start()
        load(u, 1).start()
    wload = pltpu.make_async_copy(w_hbm, w_v, wsem)
    wload.start()

    pl.semaphore_wait(barrier, sum(cond.astype(jnp.int32) for cond, _ in peers))

    last = lines - 1

    def halo_copy(u, c=None):
        src, dst, sem = right_hbm.at[line_of(u)], right_v.at[u, pl.ds(0, n)], u
        if c is not None:
            src = right_hbm.at[line_of(u), pl.ds(c * blk, blk)]
            dst, sem = right_v.at[u, pl.ds(c * blk, blk)], lines + c
        return remote(src, dst, halo_ss.at[sem], halo_rs.at[sem], dev(1, me))

    def halo_copies(u):
        return [halo_copy(u, c) for c in range(nblk)] if u == last else [halo_copy(u)]

    def send_halo(u):
        @pl.when(has_r)
        def _():
            for copy in halo_copies(u):
                copy.start()

    send_halo(0)

    def mt_up(u):
        return remote(own_mt.at[u], halo_in.at[u], mt_ss.at[u, 0], mt_rs.at[u, 0], dev(1, me))

    def mt_down(u, c=None):
        src, dst, sem = halo_mt.at[u], own_in.at[u], u
        if c is not None:
            cols = pl.ds(c * blk, blk)
            src, dst, sem = halo_mt.at[u, :, cols], own_in.at[u, :, cols], lines + c
        return remote(src, dst, mt_ss.at[sem, 1], mt_rs.at[sem, 1], dev(-1, me))

    def mt_downs(u):
        return [mt_down(u, c) for c in range(nblk)] if u == last else [mt_down(u)]

    def c2_up(u):
        return remote(own_c2.at[u], halo_c2_in.at[u], c2_ss.at[u, 0], c2_rs.at[u, 0], dev(1, me))

    def c2_down(u):
        return remote(halo_c2.at[u], own_c2_in.at[u], c2_ss.at[u, 1], c2_rs.at[u, 1], dev(-1, me))

    def line_routes():
        routes = []
        for u in range(lines):
            routes.append((u, u + REACH, None, 0, me))
            if u < REACH:
                routes.append((u, REACH - 1 - u, has_x, 1, cross))
            if u >= lines - REACH:
                routes.append((u, 2 * lines + REACH - 1 - u, None, 2, mate))
        return routes

    def line_copies(u_pick, slots=None, edges=None):
        copies = []
        for u, slot, cond, to, ln in line_routes():
            if u_pick is not None and u != u_pick or slots is not None and slot not in slots:
                continue
            mine = u + REACH
            cond = me >= 0 if cond is None else cond
            if to and edges is not True:
                copies.append((cond, cond, remote(
                    x0.at[mine, pl.ds(PAD, n)], x0.at[slot, pl.ds(PAD, n)],
                    ln_ss.at[u, to, 0], ln_rs.at[slot, 0], dev(0, ln))))
            if edges is False:
                continue
            copies.append((cond & has_r, cond & has_l, remote(
                x0.at[mine, pl.ds(n, PAD)], x0.at[slot, pl.ds(0, PAD)],
                ln_ss.at[u, to, 1], ln_rs.at[slot, 1], dev(1, ln))))
            copies.append((cond & has_l, cond & has_r, remote(
                x0.at[mine, pl.ds(PAD, PAD)], x0.at[slot, pl.ds(n + PAD, PAD)],
                ln_ss.at[u, to, 2], ln_rs.at[slot, 2], dev(-1, ln))))
        return copies

    e_ids = lax.broadcasted_iota(jnp.int32, (2 * n, chans), 0)
    lane = lax.broadcasted_iota(jnp.int32, (2 * n, chans), 1)
    t = n - e_ids
    low = t & 7
    tcol[...] = jnp.where(
        lane == 0, 1, jnp.where(lane == 1, t - low, jnp.where(lane == 2, low, 0))
    ).astype(F32).astype(BF16)

    @pl.when(jnp.logical_not(has_l))
    def _():
        right_v[:, 0:n, :] = jnp.zeros((lines, n, chans), BF16)
        halo_in[:, 0:1, :] = jnp.full((lines, 1, n), NEG, F32)
        halo_in[:, 1:2, :] = jnp.zeros((lines, 1, n), F32)
        halo_c2_in[...] = jnp.zeros((lines, 1, n), F32)
        x0[:, 0:PAD, :] = jnp.zeros((lines + 2 * REACH, PAD, chans), BF16)

    @pl.when(jnp.logical_not(has_r))
    def _():
        own_in[:, 0:1, :] = jnp.full((lines, 1, n), NEG, F32)
        own_in[:, 1:2, :] = jnp.zeros((lines, 1, n), F32)
        own_c2_in[...] = jnp.zeros((lines, 1, n), F32)
        x0[:, n + PAD : wide, :] = jnp.zeros((lines + 2 * REACH, PAD, chans), BF16)

    @pl.when(jnp.logical_not(has_x))
    def _():
        x0[0:REACH] = jnp.zeros((REACH, wide, chans), BF16)

    y_ref[:, 0:8, :] = jnp.zeros((6, 8, chans), F32)
    y_ref[:, 8 + wide : 16 + wide, :] = jnp.zeros((6, 8, chans), F32)

    il = lax.broadcasted_iota(jnp.int32, (blk // 2, blk), 0)
    jl = lax.broadcasted_iota(jnp.int32, (blk // 2, blk), 1)

    def partial_lse(u, own, chunks=tuple(range(nblk))):
        base = n if own else 0
        dst = own_mt if own else halo_mt
        for c in chunks:
            cols = right_v[u, base + c * blk : base + (c + 1) * blk, :]
            pieces = []
            top = jnp.full((8, blk), NEG, F32)
            for r in range(c, nblk) if own else range(c + 1):
                at = base + (c - r) * blk
                for h in range(2):
                    rows = slice(r * blk + h * (blk // 2), r * blk + (h + 1) * (blk // 2))
                    s = nt_dot(left_v[u, rows, :], cols) * scale
                    if r == c:
                        ih = il + h * (blk // 2)
                        s = jnp.where(jl <= ih if own else jl > ih, s, NEG)
                    s_ref[u, rows, at : at + blk] = s
                    top = jnp.maximum(top, jnp.max(groups(s), axis=0))
                    pieces.append((rows, at))
            total = jnp.zeros((8, blk), F32)
            for rows, at in pieces:
                g = groups(s_ref[u, rows, at : at + blk])
                total = total + jnp.sum(jnp.exp2(g - top[None]), axis=0)
            m = jnp.max(top, axis=0, keepdims=True)
            dst[u, 0:1, c * blk : (c + 1) * blk] = m
            dst[u, 1:2, c * blk : (c + 1) * blk] = jnp.sum(
                total * jnp.exp2(top - m), axis=0, keepdims=True
            )

    def col_pot(a, b):
        m = jnp.maximum(a[0:1], b[0:1])
        tot = a[1:2] * jnp.exp2(a[0:1] - m) + b[1:2] * jnp.exp2(b[0:1] - m)
        return -(m + jnp.log(tot) * LOG2E)

    rows_at = min(128, blk)
    steps = n // rows_at
    tiles = [slice(j * 128, min(win, (j + 1) * 128)) for j in range(-(-win // 128))]

    def pot_at(k):
        return pl.multiple_of((k * rows_at) // blk * blk, blk)

    def row_max(u, k):
        here = pl.ds(pl.multiple_of(k * rows_at, rows_at), rows_at)
        top = None
        for tile in tiles:
            width = tile.stop - tile.start
            pot = c1[:, pl.ds(pot_at(k) + tile.start, width)]
            t = groups(s_ref[u, here, tile]) + pot[None]
            if width < 128:
                t = jnp.concatenate([t] * (128 // width), axis=2)
            top = t if top is None else jnp.maximum(top, t)
        return jnp.broadcast_to(jnp.max(top, axis=2, keepdims=True), top.shape)

    def row_exp(u, k, top):
        here = pl.ds(pl.multiple_of(k * rows_at, rows_at), rows_at)
        total = None
        for tile in tiles:
            width = tile.stop - tile.start
            pot = c1[:, pl.ds(pot_at(k) + tile.start, width)]
            t = groups(s_ref[u, here, tile]) + pot[None]
            e = jnp.exp2(t - top[:, :, :width])
            k_ref[u % 3, here, tile] = e.reshape(rows_at, width)
            if width < 128:
                e = jnp.concatenate([e, jnp.zeros(e.shape[:2] + (128 - width,), F32)], axis=2)
            total = e if total is None else total + e
        return jnp.broadcast_to(1.0 / jnp.sum(total, axis=2, keepdims=True), total.shape)

    def col_sum(u, k, inv):
        here = pl.ds(pl.multiple_of(k * rows_at, rows_at), rows_at)
        for tile in tiles:
            width = tile.stop - tile.start
            part = jnp.sum(groups(k_ref[u % 3, here, tile]) * inv[:, :, :width], axis=0)
            c2acc[:, pl.ds(pot_at(k) + tile.start, width)] += part

    def row_halo(u):
        halo = jnp.where(has_l, col_pot(halo_mt[u], halo_in[u]), NEG)
        c1[:, 0:n] = jnp.broadcast_to(halo, (8, n))
        c2acc[...] = jnp.zeros((8, 2 * n), F32)

    def row_own(u, c0, c1_):
        cols = slice(c0 * blk, c1_ * blk)
        own = col_pot(own_mt[u, :, cols], own_in[u, :, cols])
        c1[:, n + c0 * blk : n + c1_ * blk] = jnp.broadcast_to(own, (8, (c1_ - c0) * blk))

    def row_rows(u, first, stop):
        inv = row_exp(u, first, row_max(u, first))
        top = row_max(u, first + 1)

        def step(k, carry):
            top, inv = carry
            col_sum(u, k - 2, inv)
            inv = row_exp(u, k - 1, top)
            return row_max(u, k), inv

        if stop > first + 2:
            top, inv = lax.fori_loop(first + 2, stop, step, (top, inv))
        col_sum(u, stop - 2, inv)
        col_sum(u, stop - 1, row_exp(u, stop - 1, top))

    def row_done(u):
        halo_c2[u] = jnp.sum(c2acc[:, 0:n], axis=0, keepdims=True)
        own_c2[u] = jnp.sum(c2acc[:, n : 2 * n], axis=0, keepdims=True)

    def transport(u):
        c1[:, n : 2 * n] = jnp.broadcast_to(1.0 / (own_c2[u] + own_c2_in[u]), (8, n))
        c1[:, 0:n] = jnp.broadcast_to(
            jnp.where(has_l, 1.0 / (halo_c2[u] + halo_c2_in[u]), 0.0), (8, n)
        )
        ln = line_of(u)

        for at in range(0, n, blk):
            q = groups(k_ref[u % 3, pl.ds(at, blk), :]) * c1[:, pl.ds(at, win)][None]
            q = q.reshape(blk, win).astype(BF16)
            rhs = jnp.concatenate([right_v[u, pl.ds(at, win), :], tcol[pl.ds(at, win), :]], axis=1)
            o = jnp.dot(q, rhs, preferred_element_type=F32)
            matched = o[:, :chans] * (1.0 / o[:, chans : chans + 1])
            x0[u + REACH, pl.ds(PAD + at, blk), :] = (
                matched - left_v[u, pl.ds(at, blk), :].astype(F32)
            ).astype(BF16)
            rowed = jnp.transpose(o[:, chans:])
            ids = (lax.broadcasted_iota(jnp.int32, (1, blk), 1) + at).astype(F32)
            disp_ref[pl.ds(ln, 1), pl.ds(at, blk)] = ids + (rowed[1:2] + rowed[2:3]) / rowed[0:1]

    def own_step(u, carry):
        load(u, 0).wait()
        load(u, 1).wait()
        partial_lse(u, True)

        @pl.when(has_r)
        def _():
            mt_up(u).start()

        return carry

    lax.fori_loop(0, lines, own_step, 0)
    send_halo(1)

    wload.wait()
    wbig[...] = jnp.zeros(wbig.shape, BF16)
    for k in range(layers):
        for a in range(3):
            tap = a + core * (2 - 2 * a)
            for b in range(3):
                w = w_v[k, tap, b]
                for h in range(2):
                    wbig[k, (a + h) * chans : (a + h + 1) * chans,
                         (3 * h + b) * chans : (3 * h + b + 1) * chans] = w

    def scores_step(u):
        for i, (copy, send) in enumerate(zip(halo_copies(u), mt_downs(u))):
            @pl.when(has_l)
            def _():
                copy.wait_recv()

            partial_lse(u, False, (i,) if u == last else tuple(range(nblk)))

            @pl.when(has_l)
            def _():
                send.start()

    def send_c2(u):
        row_done(u)

        @pl.when(has_r)
        def _():
            c2_up(u).start()

        @pl.when(has_l)
        def _():
            c2_down(u).start()

    def row_first(u):
        @pl.when(has_l)
        def _():
            mt_up(u).wait_recv()

        row_halo(u)

    def mt_arrived(copies):
        @pl.when(has_r)
        def _():
            for copy in copies:
                copy.wait_recv()

    def row_step(u):
        row_first(u)
        mt_arrived(mt_downs(u))
        row_own(u, 0, nblk)
        row_rows(u, 0, steps)
        send_c2(u)

    def plan_step(u):
        @pl.when(has_l)
        def _():
            c2_up(u).wait_recv()

        @pl.when(has_r)
        def _():
            c2_down(u).wait_recv()

        transport(u)
        for cond, _, copy in line_copies(u):
            @pl.when(cond)
            def _():
                copy.start()

    def wait_slots(slots, edges):
        for _, cond, copy in line_copies(None, slots, edges):
            @pl.when(cond)
            def _():
                copy.wait_recv()

    part = wide // 3 if (wide // 3) % 16 == 0 else wide
    step_rows = 96

    def conv_pair(src, k, slot, store, new_slots=()):
        count = wide // part
        for i in range(count):
            if i == 1 and new_slots:
                wait_slots(new_slots, True)
            g = (i + count // 2) % count
            rows = slice(g * part, (g + 1) * part)
            ins = jnp.concatenate([src[slot - 1 + i, rows, :] for i in range(4)], axis=1)
            y = jnp.dot(ins, wbig[k], preferred_element_type=F32)
            for j in range(6):
                y_ref[j, 8 + g * part : 8 + (g + 1) * part, :] = y[:, j * chans : (j + 1) * chans]
        for h in range(2):
            store(h, src, slot + h, bias_ref[k : k + 1, :])

    def updated(h, src, slot, bias, at, rows):
        total = (
            y_ref[3 * h, 7 + at : 7 + at + rows, :]
            + y_ref[3 * h + 1, 8 + at : 8 + at + rows, :]
            + y_ref[3 * h + 2, 9 + at : 9 + at + rows, :]
        )
        state = src[slot, at : at + rows, :].astype(F32)
        return (state + jnp.maximum(total + bias, 0.0)).astype(BF16)

    def clear_edges(dst, first, last):
        @pl.when(jnp.logical_not(has_l))
        def _():
            dst[first:last, 0:PAD, :] = jnp.zeros((last - first, PAD, chans), BF16)

        @pl.when(jnp.logical_not(has_r))
        def _():
            dst[first:last, n + PAD : wide, :] = jnp.zeros((last - first, PAD, chans), BF16)

        if first < REACH:
            stop = min(last, REACH)

            @pl.when(jnp.logical_not(has_x))
            def _():
                dst[first:stop] = jnp.zeros((stop - first, wide, chans), BF16)

    def layer_pair(src, dst, k, first, new_slots=()):
        wait_slots(new_slots, False)

        def keep(h, src, slot, bias):
            for at in range(0, wide, step_rows):
                dst[slot, at : at + step_rows, :] = updated(h, src, slot, bias, at, step_rows)

        conv_pair(src, k, first, keep, new_slots)
        clear_edges(dst, first, first + 2)

    def put(h, src, slot, bias):
        ln = line_of(slot - REACH)
        for at in range(0, n, 128):
            out_ref[ln, at : at + 128, :] = updated(h, src, slot, bias, at + PAD, 128)

    for u in range(lines):
        scores_step(u)
        if u >= 1:
            row_step(u - 1)
        if u + 2 < lines:
            send_halo(u + 2)
        if u >= 2 and u < last:
            plan_step(u - 2)
    per = blk // rows_at
    row_first(last)
    mt_arrived(mt_downs(last)[:-1])
    row_own(last, 0, nblk - 1)
    row_rows(last, 0, steps - per)
    mt_arrived(mt_downs(last)[-1:])
    row_own(last, nblk - 1, nblk)
    if per == 1:
        col_sum(last, steps - 1, row_exp(last, steps - 1, row_max(last, steps - 1)))
    else:
        row_rows(last, steps - per, steps)
    send_c2(last)
    plan_step(lines - 3)
    plan_step(lines - 2)
    plan_step(last)
    layer_pair(x0, x1, 0, 3, (2, 3, 4, 5))
    layer_pair(x0, x1, 0, 1, (0, 1))
    layer_pair(x1, x2, 1, 2)
    layer_pair(x0, x1, 0, 5, (6, 7))
    layer_pair(x0, x1, 0, 7, (8, 9))
    layer_pair(x1, x2, 1, 4)
    layer_pair(x1, x2, 1, 6)
    conv_pair(x2, 2, 3, put)
    conv_pair(x2, 2, 5, put)

    @pl.when(has_r)
    def _():
        for u in range(lines):
            for copy in halo_copies(u):
                copy.wait_send()
            mt_up(u).wait_send()
            c2_up(u).wait_send()

    @pl.when(has_l)
    def _():
        for u in range(lines):
            for copy in mt_downs(u):
                copy.wait_send()
            c2_down(u).wait_send()

    for cond, _, copy in line_copies(None):
        @pl.when(cond)
        def _():
            copy.wait_send()


def shards(segs, line_devs, left, right, weight, bias):
    lines, n, chans = left.shape
    layers = weight.shape[0]
    blk = n // 4
    wide = n + 2 * PAD
    slots = lines + 2 * REACH
    shape = (segs, line_devs, lines, n, blk, chans, layers)
    dma = pltpu.SemaphoreType.DMA
    vm = pltpu.VMEM
    return pl.pallas_call(
        functools.partial(body, shape),
        out_shape=(
            jax.ShapeDtypeStruct((lines, n, chans), BF16),
            jax.ShapeDtypeStruct((lines, n), F32),
        ),
        in_specs=[pl.BlockSpec(memory_space=pl.ANY)] * 3 + [pl.BlockSpec(memory_space=vm)],
        out_specs=(pl.BlockSpec(memory_space=vm), pl.BlockSpec(memory_space=vm)),
        scratch_shapes=[
            vm((lines, n, chans), BF16),
            vm((lines, 2 * n, chans), BF16),
            vm((2 * n, chans), BF16),
            vm((lines, n, n + blk), F32),
            vm((3, n, n + blk), F32),
            vm((lines, 2, n), F32),
            vm((lines, 2, n), F32),
            vm((lines, 2, n), F32),
            vm((lines, 2, n), F32),
            vm((8, 2 * n), F32),
            vm((8, 2 * n), F32),
            vm((lines, 1, n), F32),
            vm((lines, 1, n), F32),
            vm((lines, 1, n), F32),
            vm((lines, 1, n), F32),
            vm(weight.shape, BF16),
            vm((layers, 4 * chans, 6 * chans), BF16),
            vm((slots, wide, chans), BF16),
            vm((slots, wide, chans), BF16),
            vm((slots, wide, chans), BF16),
            vm((6, wide + 16, chans), F32),
            dma((lines, 2)),
            dma,
            dma((lines + 4,)),
            dma((lines + 4,)),
            dma((lines + 4, 2)),
            dma((lines + 4, 2)),
            dma((lines, 2)),
            dma((lines, 2)),
            dma((lines, 3, 3)),
            dma((slots, 3)),
        ],
        compiler_params=pltpu.CompilerParams(
            collective_id=0, has_side_effects=True, vmem_limit_bytes=60 * 1024 * 1024
        ),
        name="stereo",
    )(left, right, weight, bias)


def solution(mesh):
    return jax.shard_map(
        functools.partial(shards, mesh.shape["seg"], mesh.shape["lines"]),
        mesh=mesh,
        in_specs=(P("lines", "seg", None), P("lines", "seg", None), P(), P()),
        out_specs=(P("lines", "seg", None), P("lines", "seg")),
        check_vma=False,
    )
```

```python
import functools
import math

import jax
import jax.numpy as jnp
from jax import lax
from jax.experimental import pallas as pl
from jax.experimental.pallas import tpu as pltpu
from jax.sharding import PartitionSpec as P

NEG = -1e30
LOG2E = 1.4426950408889634
PAD = 16
REACH = 3
MESH = pl.DeviceIdType.MESH
F32 = jnp.float32
BF16 = jnp.bfloat16


def nt_dot(a, b):
    return lax.dot_general(a, b, (((1,), (1,)), ((), ())), preferred_element_type=F32)


def groups(x):
    return x.reshape(x.shape[0] // 8, 8, x.shape[1])


def body(
    shape, left_hbm, right_hbm, w_hbm, bias_ref, out_ref, disp_ref,
    left_v, right_v, tcol, s_ref, k_ref, own_mt, halo_mt, own_in, halo_in, c1, c2acc,
    own_c2, halo_c2, own_c2_in, halo_c2_in, w_v, wbig, x0, x1, x2, y_ref,
    load_sem, wsem, halo_ss, halo_rs, mt_ss, mt_rs, c2_ss, c2_rs, ln_ss, ln_rs,
):
    segs, line_devs, lines, n, blk, chans, layers = shape
    nblk = n // blk
    win = n + blk
    wide = n + 2 * PAD
    scale = LOG2E / math.sqrt(chans)
    seg = lax.axis_index("seg")
    me = lax.axis_index("lines")
    core = lax.rem(me, 2)
    mate = me + 1 - 2 * core
    cross = me - 1 + 2 * core
    has_l = seg > 0
    has_r = seg < segs - 1
    has_x = (cross >= 0) & (cross < line_devs)

    def dev(ds, ln):
        return {"seg": seg + ds, "lines": ln}

    def line_of(u):
        return u + core * (lines - 1 - 2 * u)

    def remote(src, dst, ss, rs, where):
        return pltpu.make_async_remote_copy(
            src_ref=src, dst_ref=dst, send_sem=ss, recv_sem=rs, device_id=where, device_id_type=MESH
        )

    barrier = pltpu.get_barrier_semaphore()
    peers = []
    for ds, side in ((-1, has_l), (1, has_r)):
        peers += [(side, dev(ds, me))]
    peers += [(me >= 0, dev(0, mate)), (has_x, dev(0, cross))]
    for cond, where in peers:
        @pl.when(cond)
        def _():
            pl.semaphore_signal(barrier, inc=1, device_id=where, device_id_type=MESH)

    def load(u, which):
        src = (left_hbm, right_hbm)[which].at[line_of(u)]
        dst = left_v.at[u] if which == 0 else right_v.at[u, pl.ds(n, n)]
        return pltpu.make_async_copy(src, dst, load_sem.at[u, which])

    for u in range(lines):
        load(u, 0).start()
        load(u, 1).start()
    wload = pltpu.make_async_copy(w_hbm, w_v, wsem)
    wload.start()

    pl.semaphore_wait(barrier, sum(cond.astype(jnp.int32) for cond, _ in peers))

    last = lines - 1

    def halo_copies(u):
        count = nblk if u == last else 2
        size = n // count
        return [
            remote(
                right_hbm.at[line_of(u), pl.ds(c * size, size)],
                right_v.at[u, pl.ds(c * size, size)],
                halo_ss.at[u, c], halo_rs.at[u, c], dev(1, me),
            )
            for c in range(count)
        ]

    def send_halo(u, half):
        copies = halo_copies(u)
        per_half = len(copies) // 2

        @pl.when(has_r)
        def _():
            for copy in copies[half * per_half : (half + 1) * per_half]:
                copy.start()

    send_halo(0, 0)
    send_halo(0, 1)

    def mt_up(u):
        return remote(own_mt.at[u], halo_in.at[u], mt_ss.at[u, 0], mt_rs.at[u, 0], dev(1, me))

    def mt_down(u, c=None):
        src, dst, sem = halo_mt.at[u], own_in.at[u], u
        if c is not None:
            cols = pl.ds(c * blk, blk)
            src, dst, sem = halo_mt.at[u, :, cols], own_in.at[u, :, cols], lines + c
        return remote(src, dst, mt_ss.at[sem, 1], mt_rs.at[sem, 1], dev(-1, me))

    def mt_downs(u):
        return [mt_down(u, c) for c in range(nblk)] if u == last else [mt_down(u)]

    def c2_up(u):
        return remote(own_c2.at[u], halo_c2_in.at[u], c2_ss.at[u, 0], c2_rs.at[u, 0], dev(1, me))

    def c2_down(u):
        return remote(halo_c2.at[u], own_c2_in.at[u], c2_ss.at[u, 1], c2_rs.at[u, 1], dev(-1, me))

    def line_routes():
        routes = []
        for u in range(lines):
            routes.append((u, u + REACH, None, 0, me))
            if u < REACH:
                routes.append((u, REACH - 1 - u, has_x, 1, cross))
            if u >= lines - REACH:
                routes.append((u, 2 * lines + REACH - 1 - u, None, 2, mate))
        return routes

    def line_copies(u_pick, slots=None, edges=None):
        copies = []
        for u, slot, cond, to, ln in line_routes():
            if u_pick is not None and u != u_pick or slots is not None and slot not in slots:
                continue
            mine = u + REACH
            cond = me >= 0 if cond is None else cond
            if to and edges is not True:
                copies.append((cond, cond, remote(
                    x0.at[mine, pl.ds(PAD, n)], x0.at[slot, pl.ds(PAD, n)],
                    ln_ss.at[u, to, 0], ln_rs.at[slot, 0], dev(0, ln))))
            if edges is False:
                continue
            copies.append((cond & has_r, cond & has_l, remote(
                x0.at[mine, pl.ds(n, PAD)], x0.at[slot, pl.ds(0, PAD)],
                ln_ss.at[u, to, 1], ln_rs.at[slot, 1], dev(1, ln))))
            copies.append((cond & has_l, cond & has_r, remote(
                x0.at[mine, pl.ds(PAD, PAD)], x0.at[slot, pl.ds(n + PAD, PAD)],
                ln_ss.at[u, to, 2], ln_rs.at[slot, 2], dev(-1, ln))))
        return copies

    e_ids = lax.broadcasted_iota(jnp.int32, (2 * n, chans), 0)
    lane = lax.broadcasted_iota(jnp.int32, (2 * n, chans), 1)
    t = n - e_ids
    low = t & 7
    tcol[...] = jnp.where(
        lane == 0, 1, jnp.where(lane == 1, t - low, jnp.where(lane == 2, low, 0))
    ).astype(F32).astype(BF16)

    @pl.when(jnp.logical_not(has_l))
    def _():
        right_v[:, 0:n, :] = jnp.zeros((lines, n, chans), BF16)
        halo_in[:, 0:1, :] = jnp.full((lines, 1, n), NEG, F32)
        halo_in[:, 1:2, :] = jnp.zeros((lines, 1, n), F32)
        halo_c2_in[...] = jnp.zeros((lines, 1, n), F32)
        x0[:, 0:PAD, :] = jnp.zeros((lines + 2 * REACH, PAD, chans), BF16)

    @pl.when(jnp.logical_not(has_r))
    def _():
        own_in[:, 0:1, :] = jnp.full((lines, 1, n), NEG, F32)
        own_in[:, 1:2, :] = jnp.zeros((lines, 1, n), F32)
        own_c2_in[...] = jnp.zeros((lines, 1, n), F32)
        x0[:, n + PAD : wide, :] = jnp.zeros((lines + 2 * REACH, PAD, chans), BF16)

    @pl.when(jnp.logical_not(has_x))
    def _():
        x0[0:REACH] = jnp.zeros((REACH, wide, chans), BF16)

    y_ref[:, 0:8, :] = jnp.zeros((6, 8, chans), F32)
    y_ref[:, 8 + wide : 16 + wide, :] = jnp.zeros((6, 8, chans), F32)

    il = lax.broadcasted_iota(jnp.int32, (blk // 2, blk), 0)
    jl = lax.broadcasted_iota(jnp.int32, (blk // 2, blk), 1)

    def partial_lse(u, own, chunks=tuple(range(nblk))):
        base = n if own else 0
        dst = own_mt if own else halo_mt
        for c in chunks:
            cols = right_v[u, base + c * blk : base + (c + 1) * blk, :]
            pieces = []
            top = jnp.full((8, blk), NEG, F32)
            for r in range(c, nblk) if own else range(c + 1):
                at = base + (c - r) * blk
                for h in range(2):
                    rows = slice(r * blk + h * (blk // 2), r * blk + (h + 1) * (blk // 2))
                    s = nt_dot(left_v[u, rows, :], cols) * scale
                    if r == c:
                        ih = il + h * (blk // 2)
                        s = jnp.where(jl <= ih if own else jl > ih, s, NEG)
                    s_ref[u, rows, at : at + blk] = s
                    top = jnp.maximum(top, jnp.max(groups(s), axis=0))
                    pieces.append((rows, at))
            total = jnp.zeros((8, blk), F32)
            for rows, at in pieces:
                g = groups(s_ref[u, rows, at : at + blk])
                total = total + jnp.sum(jnp.exp2(g - top[None]), axis=0)
            m = jnp.max(top, axis=0, keepdims=True)
            dst[u, 0:1, c * blk : (c + 1) * blk] = m
            dst[u, 1:2, c * blk : (c + 1) * blk] = jnp.sum(
                total * jnp.exp2(top - m), axis=0, keepdims=True
            )

    def col_pot(a, b):
        m = jnp.maximum(a[0:1], b[0:1])
        tot = a[1:2] * jnp.exp2(a[0:1] - m) + b[1:2] * jnp.exp2(b[0:1] - m)
        return -(m + jnp.log(tot) * LOG2E)

    rows_at = min(128, blk)
    steps = n // rows_at
    tiles = [slice(j * 128, min(win, (j + 1) * 128)) for j in range(-(-win // 128))]

    def pot_at(k):
        return pl.multiple_of((k * rows_at) // blk * blk, blk)

    def row_max(u, k):
        here = pl.ds(pl.multiple_of(k * rows_at, rows_at), rows_at)
        top = None
        for tile in tiles:
            width = tile.stop - tile.start
            pot = c1[:, pl.ds(pot_at(k) + tile.start, width)]
            t = groups(s_ref[u, here, tile]) + pot[None]
            if width < 128:
                t = jnp.concatenate([t] * (128 // width), axis=2)
            top = t if top is None else jnp.maximum(top, t)
        return jnp.broadcast_to(jnp.max(top, axis=2, keepdims=True), top.shape)

    def row_exp(u, k, top):
        here = pl.ds(pl.multiple_of(k * rows_at, rows_at), rows_at)
        total = None
        for tile in tiles:
            width = tile.stop - tile.start
            pot = c1[:, pl.ds(pot_at(k) + tile.start, width)]
            t = groups(s_ref[u, here, tile]) + pot[None]
            e = jnp.exp2(t - top[:, :, :width])
            k_ref[u % 3, here, tile] = e.reshape(rows_at, width)
            if width < 128:
                e = jnp.concatenate([e, jnp.zeros(e.shape[:2] + (128 - width,), F32)], axis=2)
            total = e if total is None else total + e
        return jnp.broadcast_to(1.0 / jnp.sum(total, axis=2, keepdims=True), total.shape)

    def col_sum(u, k, inv):
        here = pl.ds(pl.multiple_of(k * rows_at, rows_at), rows_at)
        for tile in tiles:
            width = tile.stop - tile.start
            part = jnp.sum(groups(k_ref[u % 3, here, tile]) * inv[:, :, :width], axis=0)
            c2acc[:, pl.ds(pot_at(k) + tile.start, width)] += part

    def row_halo(u):
        halo = jnp.where(has_l, col_pot(halo_mt[u], halo_in[u]), NEG)
        c1[:, 0:n] = jnp.broadcast_to(halo, (8, n))
        c2acc[...] = jnp.zeros((8, 2 * n), F32)

    def row_own(u, c0, c1_):
        cols = slice(c0 * blk, c1_ * blk)
        own = col_pot(own_mt[u, :, cols], own_in[u, :, cols])
        c1[:, n + c0 * blk : n + c1_ * blk] = jnp.broadcast_to(own, (8, (c1_ - c0) * blk))

    def row_rows(u, first, stop):
        inv = row_exp(u, first, row_max(u, first))
        top = row_max(u, first + 1)

        def step(k, carry):
            top, inv = carry
            col_sum(u, k - 2, inv)
            inv = row_exp(u, k - 1, top)
            return row_max(u, k), inv

        if stop > first + 2:
            top, inv = lax.fori_loop(first + 2, stop, step, (top, inv))
        col_sum(u, stop - 2, inv)
        col_sum(u, stop - 1, row_exp(u, stop - 1, top))

    def row_done(u):
        halo_c2[u] = jnp.sum(c2acc[:, 0:n], axis=0, keepdims=True)
        own_c2[u] = jnp.sum(c2acc[:, n : 2 * n], axis=0, keepdims=True)

    def transport(u):
        c1[:, n : 2 * n] = jnp.broadcast_to(1.0 / (own_c2[u] + own_c2_in[u]), (8, n))
        c1[:, 0:n] = jnp.broadcast_to(
            jnp.where(has_l, 1.0 / (halo_c2[u] + halo_c2_in[u]), 0.0), (8, n)
        )
        ln = line_of(u)

        for at in range(0, n, blk):
            q = groups(k_ref[u % 3, pl.ds(at, blk), :]) * c1[:, pl.ds(at, win)][None]
            q = q.reshape(blk, win).astype(BF16)
            rhs = jnp.concatenate([right_v[u, pl.ds(at, win), :], tcol[pl.ds(at, win), :]], axis=1)
            o = jnp.dot(q, rhs, preferred_element_type=F32)
            matched = o[:, :chans] * (1.0 / o[:, chans : chans + 1])
            x0[u + REACH, pl.ds(PAD + at, blk), :] = (
                matched - left_v[u, pl.ds(at, blk), :].astype(F32)
            ).astype(BF16)
            rowed = jnp.transpose(o[:, chans:])
            ids = (lax.broadcasted_iota(jnp.int32, (1, blk), 1) + at).astype(F32)
            disp_ref[pl.ds(ln, 1), pl.ds(at, blk)] = ids + (rowed[1:2] + rowed[2:3]) / rowed[0:1]

    def own_step(u, carry):
        load(u, 0).wait()
        load(u, 1).wait()
        partial_lse(u, True)

        @pl.when(has_r)
        def _():
            mt_up(u).start()

        return carry

    lax.fori_loop(0, lines, own_step, 0)
    send_halo(1, 0)

    wload.wait()
    wbig[...] = jnp.zeros(wbig.shape, BF16)
    for k in range(layers):
        for a in range(3):
            tap = a + core * (2 - 2 * a)
            for b in range(3):
                w = w_v[k, tap, b]
                for h in range(2):
                    wbig[k, (a + h) * chans : (a + h + 1) * chans,
                         (3 * h + b) * chans : (3 * h + b + 1) * chans] = w

    def scores_step(u):
        halves = halo_copies(u)
        sends = mt_downs(u)
        per_send = len(halves) // len(sends)
        for i, send in enumerate(sends):
            @pl.when(has_l)
            def _():
                for copy in halves[i * per_send : (i + 1) * per_send]:
                    copy.wait_recv()

            partial_lse(u, False, (i,) if u == last else tuple(range(nblk)))

            @pl.when(has_l)
            def _():
                send.start()

    def send_c2(u):
        row_done(u)

        @pl.when(has_r)
        def _():
            c2_up(u).start()

        @pl.when(has_l)
        def _():
            c2_down(u).start()

    def row_first(u):
        @pl.when(has_l)
        def _():
            mt_up(u).wait_recv()

        row_halo(u)

    def mt_arrived(copies):
        @pl.when(has_r)
        def _():
            for copy in copies:
                copy.wait_recv()

    def row_step(u):
        row_first(u)
        mt_arrived(mt_downs(u))
        row_own(u, 0, nblk)
        row_rows(u, 0, steps)
        send_c2(u)

    def plan_step(u):
        @pl.when(has_l)
        def _():
            c2_up(u).wait_recv()

        @pl.when(has_r)
        def _():
            c2_down(u).wait_recv()

        transport(u)
        for cond, _, copy in line_copies(u):
            @pl.when(cond)
            def _():
                copy.start()

    def wait_slots(slots, edges):
        for _, cond, copy in line_copies(None, slots, edges):
            @pl.when(cond)
            def _():
                copy.wait_recv()

    part = wide // 3 if (wide // 3) % 16 == 0 else wide
    step_rows = 96

    def conv_pair(src, k, slot, store, new_slots=()):
        count = wide // part
        for i in range(count):
            if i == 1 and new_slots:
                wait_slots(new_slots, True)
            g = (i + count // 2) % count
            rows = slice(g * part, (g + 1) * part)
            ins = jnp.concatenate([src[slot - 1 + i, rows, :] for i in range(4)], axis=1)
            y = jnp.dot(ins, wbig[k], preferred_element_type=F32)
            for j in range(6):
                y_ref[j, 8 + g * part : 8 + (g + 1) * part, :] = y[:, j * chans : (j + 1) * chans]
        for h in range(2):
            store(h, src, slot + h, bias_ref[k : k + 1, :])

    def updated(h, src, slot, bias, at, rows):
        total = (
            y_ref[3 * h, 7 + at : 7 + at + rows, :]
            + y_ref[3 * h + 1, 8 + at : 8 + at + rows, :]
            + y_ref[3 * h + 2, 9 + at : 9 + at + rows, :]
        )
        state = src[slot, at : at + rows, :].astype(F32)
        return (state + jnp.maximum(total + bias, 0.0)).astype(BF16)

    def clear_edges(dst, first, last):
        @pl.when(jnp.logical_not(has_l))
        def _():
            dst[first:last, 0:PAD, :] = jnp.zeros((last - first, PAD, chans), BF16)

        @pl.when(jnp.logical_not(has_r))
        def _():
            dst[first:last, n + PAD : wide, :] = jnp.zeros((last - first, PAD, chans), BF16)

        if first < REACH:
            stop = min(last, REACH)

            @pl.when(jnp.logical_not(has_x))
            def _():
                dst[first:stop] = jnp.zeros((stop - first, wide, chans), BF16)

    def layer_pair(src, dst, k, first, new_slots=()):
        wait_slots(new_slots, False)

        def keep(h, src, slot, bias):
            for at in range(0, wide, step_rows):
                dst[slot, at : at + step_rows, :] = updated(h, src, slot, bias, at, step_rows)

        conv_pair(src, k, first, keep, new_slots)
        clear_edges(dst, first, first + 2)

    def put(h, src, slot, bias):
        ln = line_of(slot - REACH)
        for at in range(0, n, 128):
            out_ref[ln, at : at + 128, :] = updated(h, src, slot, bias, at + PAD, 128)

    scores_step(0)
    send_halo(1, 1)
    send_halo(2, 0)
    scores_step(1)
    send_halo(2, 1)
    row_step(0)
    send_halo(3, 0)
    scores_step(2)
    send_halo(3, 1)
    row_step(1)
    plan_step(0)
    scores_step(3)
    row_step(2)
    plan_step(1)
    per = blk // rows_at
    row_first(last)
    mt_arrived(mt_downs(last)[:-1])
    row_own(last, 0, nblk - 1)
    row_rows(last, 0, steps - per)
    mt_arrived(mt_downs(last)[-1:])
    row_own(last, nblk - 1, nblk)
    if per == 1:
        col_sum(last, steps - 1, row_exp(last, steps - 1, row_max(last, steps - 1)))
    else:
        row_rows(last, steps - per, steps)
    send_c2(last)
    plan_step(2)
    plan_step(3)
    layer_pair(x0, x1, 0, 3, (2, 3, 4, 5))
    layer_pair(x0, x1, 0, 1, (0, 1))
    layer_pair(x1, x2, 1, 2)
    layer_pair(x0, x1, 0, 5, (6, 7))
    layer_pair(x0, x1, 0, 7, (8, 9))
    layer_pair(x1, x2, 1, 4)
    layer_pair(x1, x2, 1, 6)
    conv_pair(x2, 2, 3, put)
    conv_pair(x2, 2, 5, put)

    @pl.when(has_r)
    def _():
        for u in range(lines):
            for copy in halo_copies(u):
                copy.wait_send()
            mt_up(u).wait_send()
            c2_up(u).wait_send()

    @pl.when(has_l)
    def _():
        for u in range(lines):
            for copy in mt_downs(u):
                copy.wait_send()
            c2_down(u).wait_send()

    for cond, _, copy in line_copies(None):
        @pl.when(cond)
        def _():
            copy.wait_send()


def shards(segs, line_devs, left, right, weight, bias):
    lines, n, chans = left.shape
    layers = weight.shape[0]
    blk = n // 4
    wide = n + 2 * PAD
    slots = lines + 2 * REACH
    shape = (segs, line_devs, lines, n, blk, chans, layers)
    dma = pltpu.SemaphoreType.DMA
    vm = pltpu.VMEM
    return pl.pallas_call(
        functools.partial(body, shape),
        out_shape=(
            jax.ShapeDtypeStruct((lines, n, chans), BF16),
            jax.ShapeDtypeStruct((lines, n), F32),
        ),
        in_specs=[pl.BlockSpec(memory_space=pl.ANY)] * 3 + [pl.BlockSpec(memory_space=vm)],
        out_specs=(pl.BlockSpec(memory_space=vm), pl.BlockSpec(memory_space=vm)),
        scratch_shapes=[
            vm((lines, n, chans), BF16),
            vm((lines, 2 * n, chans), BF16),
            vm((2 * n, chans), BF16),
            vm((lines, n, n + blk), F32),
            vm((3, n, n + blk), F32),
            vm((lines, 2, n), F32),
            vm((lines, 2, n), F32),
            vm((lines, 2, n), F32),
            vm((lines, 2, n), F32),
            vm((8, 2 * n), F32),
            vm((8, 2 * n), F32),
            vm((lines, 1, n), F32),
            vm((lines, 1, n), F32),
            vm((lines, 1, n), F32),
            vm((lines, 1, n), F32),
            vm(weight.shape, BF16),
            vm((layers, 4 * chans, 6 * chans), BF16),
            vm((slots, wide, chans), BF16),
            vm((slots, wide, chans), BF16),
            vm((slots, wide, chans), BF16),
            vm((6, wide + 16, chans), F32),
            dma((lines, 2)),
            dma,
            dma((lines, 4)),
            dma((lines, 4)),
            dma((lines + 4, 2)),
            dma((lines + 4, 2)),
            dma((lines, 2)),
            dma((lines, 2)),
            dma((lines, 3, 3)),
            dma((slots, 3)),
        ],
        compiler_params=pltpu.CompilerParams(
            collective_id=0, has_side_effects=True, vmem_limit_bytes=60 * 1024 * 1024
        ),
        name="stereo",
    )(left, right, weight, bias)


def solution(mesh):
    return jax.shard_map(
        functools.partial(shards, mesh.shape["seg"], mesh.shape["lines"]),
        mesh=mesh,
        in_specs=(P("lines", "seg", None), P("lines", "seg", None), P(), P()),
        out_specs=(P("lines", "seg", None), P("lines", "seg")),
        check_vma=False,
    )
```

```python
import functools
import math

import jax
import jax.numpy as jnp
from jax import lax
from jax.experimental import pallas as pl
from jax.experimental.pallas import tpu as pltpu
from jax.sharding import PartitionSpec as P

NEG = -1e30
LOG2E = 1.4426950408889634
PAD = 16
REACH = 3
MESH = pl.DeviceIdType.MESH
F32 = jnp.float32
BF16 = jnp.bfloat16


def nt_dot(a, b):
    return lax.dot_general(a, b, (((1,), (1,)), ((), ())), preferred_element_type=F32)


def groups(x):
    return x.reshape(x.shape[0] // 8, 8, x.shape[1])


def body(
    shape, left_hbm, right_hbm, w_hbm, bias_ref, out_hbm, disp_hbm,
    left_v, right_v, tcol, s_ref, k_ref, own_mt, halo_mt, own_in, halo_in, c1, c2acc,
    own_c2, halo_c2, own_c2_in, halo_c2_in, w_v, wbig, x0, x1, x2, y_ref,
    load_sem, wsem, halo_ss, halo_rs, mt_ss, mt_rs, c2_ss, c2_rs, ln_ss, ln_rs,
    out_ref, disp_ref, out_sem,
):
    segs, line_devs, lines, n, blk, chans, layers = shape
    nblk = n // blk
    win = n + blk
    wide = n + 2 * PAD
    scale = LOG2E / math.sqrt(chans)
    seg = lax.axis_index("seg")
    me = lax.axis_index("lines")
    core = lax.rem(me, 2)
    mate = me + 1 - 2 * core
    cross = me - 1 + 2 * core
    has_l = seg > 0
    has_r = seg < segs - 1
    has_x = (cross >= 0) & (cross < line_devs)

    def dev(ds, ln):
        return {"seg": seg + ds, "lines": ln}

    def line_of(u):
        return u + core * (lines - 1 - 2 * u)

    def remote(src, dst, ss, rs, where):
        return pltpu.make_async_remote_copy(
            src_ref=src, dst_ref=dst, send_sem=ss, recv_sem=rs, device_id=where, device_id_type=MESH
        )

    barrier = pltpu.get_barrier_semaphore()
    peers = []
    for ds, side in ((-1, has_l), (1, has_r)):
        peers += [(side, dev(ds, me))]
    peers += [(me >= 0, dev(0, mate)), (has_x, dev(0, cross))]
    for cond, where in peers:
        @pl.when(cond)
        def _():
            pl.semaphore_signal(barrier, inc=1, device_id=where, device_id_type=MESH)

    def load(u, which):
        src = (left_hbm, right_hbm)[which].at[line_of(u)]
        dst = left_v.at[u] if which == 0 else right_v.at[u, pl.ds(n, n)]
        return pltpu.make_async_copy(src, dst, load_sem.at[u, which])

    for u in range(lines):
        load(u, 0).start()
        load(u, 1).start()
    wload = pltpu.make_async_copy(w_hbm, w_v, wsem)
    wload.start()

    pl.semaphore_wait(barrier, sum(cond.astype(jnp.int32) for cond, _ in peers))

    last = lines - 1

    def halo_copies(u):
        count = nblk if u == last else 2
        size = n // count
        return [
            remote(
                right_hbm.at[line_of(u), pl.ds(c * size, size)],
                right_v.at[u, pl.ds(c * size, size)],
                halo_ss.at[u, c], halo_rs.at[u, c], dev(1, me),
            )
            for c in range(count)
        ]

    def send_halo(u, half):
        copies = halo_copies(u)
        per_half = len(copies) // 2

        @pl.when(has_r)
        def _():
            for copy in copies[half * per_half : (half + 1) * per_half]:
                copy.start()

    send_halo(0, 0)
    send_halo(0, 1)

    def mt_up(u):
        return remote(own_mt.at[u], halo_in.at[u], mt_ss.at[u, 0], mt_rs.at[u, 0], dev(1, me))

    def mt_down(u, c=None):
        src, dst, sem = halo_mt.at[u], own_in.at[u], u
        if c is not None:
            cols = pl.ds(c * blk, blk)
            src, dst, sem = halo_mt.at[u, :, cols], own_in.at[u, :, cols], lines + c
        return remote(src, dst, mt_ss.at[sem, 1], mt_rs.at[sem, 1], dev(-1, me))

    def mt_downs(u):
        return [mt_down(u, c) for c in range(nblk)] if u == last else [mt_down(u)]

    def c2_up(u):
        return remote(own_c2.at[u], halo_c2_in.at[u], c2_ss.at[u, 0], c2_rs.at[u, 0], dev(1, me))

    def c2_down(u):
        return remote(halo_c2.at[u], own_c2_in.at[u], c2_ss.at[u, 1], c2_rs.at[u, 1], dev(-1, me))

    def line_routes():
        routes = []
        for u in range(lines):
            routes.append((u, u + REACH, None, 0, me))
            if u < REACH:
                routes.append((u, REACH - 1 - u, has_x, 1, cross))
            if u >= lines - REACH:
                routes.append((u, 2 * lines + REACH - 1 - u, None, 2, mate))
        return routes

    def line_copies(u_pick, slots=None, edges=None):
        copies = []
        for u, slot, cond, to, ln in line_routes():
            if u_pick is not None and u != u_pick or slots is not None and slot not in slots:
                continue
            mine = u + REACH
            cond = me >= 0 if cond is None else cond
            if to and edges is not True:
                copies.append((cond, cond, remote(
                    x0.at[mine, pl.ds(PAD, n)], x0.at[slot, pl.ds(PAD, n)],
                    ln_ss.at[u, to, 0], ln_rs.at[slot, 0], dev(0, ln))))
            if edges is False:
                continue
            copies.append((cond & has_r, cond & has_l, remote(
                x0.at[mine, pl.ds(n, PAD)], x0.at[slot, pl.ds(0, PAD)],
                ln_ss.at[u, to, 1], ln_rs.at[slot, 1], dev(1, ln))))
            copies.append((cond & has_l, cond & has_r, remote(
                x0.at[mine, pl.ds(PAD, PAD)], x0.at[slot, pl.ds(n + PAD, PAD)],
                ln_ss.at[u, to, 2], ln_rs.at[slot, 2], dev(-1, ln))))
        return copies

    e_ids = lax.broadcasted_iota(jnp.int32, (2 * n, chans), 0)
    lane = lax.broadcasted_iota(jnp.int32, (2 * n, chans), 1)
    t = n - e_ids
    low = t & 7
    tcol[...] = jnp.where(
        lane == 0, 1, jnp.where(lane == 1, t - low, jnp.where(lane == 2, low, 0))
    ).astype(F32).astype(BF16)

    @pl.when(jnp.logical_not(has_l))
    def _():
        right_v[:, 0:n, :] = jnp.zeros((lines, n, chans), BF16)
        halo_in[:, 0:1, :] = jnp.full((lines, 1, n), NEG, F32)
        halo_in[:, 1:2, :] = jnp.zeros((lines, 1, n), F32)
        halo_c2_in[...] = jnp.zeros((lines, 1, n), F32)
        x0[:, 0:PAD, :] = jnp.zeros((lines + 2 * REACH, PAD, chans), BF16)

    @pl.when(jnp.logical_not(has_r))
    def _():
        own_in[:, 0:1, :] = jnp.full((lines, 1, n), NEG, F32)
        own_in[:, 1:2, :] = jnp.zeros((lines, 1, n), F32)
        own_c2_in[...] = jnp.zeros((lines, 1, n), F32)
        x0[:, n + PAD : wide, :] = jnp.zeros((lines + 2 * REACH, PAD, chans), BF16)

    @pl.when(jnp.logical_not(has_x))
    def _():
        x0[0:REACH] = jnp.zeros((REACH, wide, chans), BF16)

    y_ref[:, 0:8, :] = jnp.zeros((6, 8, chans), F32)
    y_ref[:, 8 + wide : 16 + wide, :] = jnp.zeros((6, 8, chans), F32)

    il = lax.broadcasted_iota(jnp.int32, (blk // 2, blk), 0)
    jl = lax.broadcasted_iota(jnp.int32, (blk // 2, blk), 1)

    def partial_lse(u, own, chunks=tuple(range(nblk))):
        base = n if own else 0
        dst = own_mt if own else halo_mt
        for c in chunks:
            cols = right_v[u, base + c * blk : base + (c + 1) * blk, :]
            pieces = []
            top = jnp.full((8, blk), NEG, F32)
            for r in range(c, nblk) if own else range(c + 1):
                at = base + (c - r) * blk
                for h in range(2):
                    rows = slice(r * blk + h * (blk // 2), r * blk + (h + 1) * (blk // 2))
                    s = nt_dot(left_v[u, rows, :], cols) * scale
                    if r == c:
                        ih = il + h * (blk // 2)
                        s = jnp.where(jl <= ih if own else jl > ih, s, NEG)
                    s_ref[u, rows, at : at + blk] = s
                    top = jnp.maximum(top, jnp.max(groups(s), axis=0))
                    pieces.append((rows, at))
            total = jnp.zeros((8, blk), F32)
            for rows, at in pieces:
                g = groups(s_ref[u, rows, at : at + blk])
                total = total + jnp.sum(jnp.exp2(g - top[None]), axis=0)
            m = jnp.max(top, axis=0, keepdims=True)
            dst[u, 0:1, c * blk : (c + 1) * blk] = m
            dst[u, 1:2, c * blk : (c + 1) * blk] = jnp.sum(
                total * jnp.exp2(top - m), axis=0, keepdims=True
            )

    def col_pot(a, b):
        m = jnp.maximum(a[0:1], b[0:1])
        tot = a[1:2] * jnp.exp2(a[0:1] - m) + b[1:2] * jnp.exp2(b[0:1] - m)
        return -(m + jnp.log(tot) * LOG2E)

    rows_at = min(128, blk)
    steps = n // rows_at
    tiles = [slice(j * 128, min(win, (j + 1) * 128)) for j in range(-(-win // 128))]

    def pot_at(k):
        return pl.multiple_of((k * rows_at) // blk * blk, blk)

    def row_max(u, k):
        here = pl.ds(pl.multiple_of(k * rows_at, rows_at), rows_at)
        top = None
        for tile in tiles:
            width = tile.stop - tile.start
            pot = c1[:, pl.ds(pot_at(k) + tile.start, width)]
            t = groups(s_ref[u, here, tile]) + pot[None]
            if width < 128:
                t = jnp.concatenate([t] * (128 // width), axis=2)
            top = t if top is None else jnp.maximum(top, t)
        return jnp.broadcast_to(jnp.max(top, axis=2, keepdims=True), top.shape)

    def row_exp(u, k, top):
        here = pl.ds(pl.multiple_of(k * rows_at, rows_at), rows_at)
        total = None
        for tile in tiles:
            width = tile.stop - tile.start
            pot = c1[:, pl.ds(pot_at(k) + tile.start, width)]
            t = groups(s_ref[u, here, tile]) + pot[None]
            e = jnp.exp2(t - top[:, :, :width])
            k_ref[u % 3, here, tile] = e.reshape(rows_at, width)
            if width < 128:
                e = jnp.concatenate([e, jnp.zeros(e.shape[:2] + (128 - width,), F32)], axis=2)
            total = e if total is None else total + e
        return jnp.broadcast_to(1.0 / jnp.sum(total, axis=2, keepdims=True), total.shape)

    def col_sum(u, k, inv):
        here = pl.ds(pl.multiple_of(k * rows_at, rows_at), rows_at)
        for tile in tiles:
            width = tile.stop - tile.start
            part = jnp.sum(groups(k_ref[u % 3, here, tile]) * inv[:, :, :width], axis=0)
            c2acc[:, pl.ds(pot_at(k) + tile.start, width)] += part

    def row_halo(u):
        halo = jnp.where(has_l, col_pot(halo_mt[u], halo_in[u]), NEG)
        c1[:, 0:n] = jnp.broadcast_to(halo, (8, n))
        c2acc[...] = jnp.zeros((8, 2 * n), F32)

    def row_own(u, c0, c1_):
        cols = slice(c0 * blk, c1_ * blk)
        own = col_pot(own_mt[u, :, cols], own_in[u, :, cols])
        c1[:, n + c0 * blk : n + c1_ * blk] = jnp.broadcast_to(own, (8, (c1_ - c0) * blk))

    def row_rows(u, first, stop):
        inv = row_exp(u, first, row_max(u, first))
        top = row_max(u, first + 1)

        def step(k, carry):
            top, inv = carry
            col_sum(u, k - 2, inv)
            inv = row_exp(u, k - 1, top)
            return row_max(u, k), inv

        if stop > first + 2:
            top, inv = lax.fori_loop(first + 2, stop, step, (top, inv))
        col_sum(u, stop - 2, inv)
        col_sum(u, stop - 1, row_exp(u, stop - 1, top))

    def row_done(u):
        halo_c2[u] = jnp.sum(c2acc[:, 0:n], axis=0, keepdims=True)
        own_c2[u] = jnp.sum(c2acc[:, n : 2 * n], axis=0, keepdims=True)

    def transport(u):
        c1[:, n : 2 * n] = jnp.broadcast_to(1.0 / (own_c2[u] + own_c2_in[u]), (8, n))
        c1[:, 0:n] = jnp.broadcast_to(
            jnp.where(has_l, 1.0 / (halo_c2[u] + halo_c2_in[u]), 0.0), (8, n)
        )
        ln = line_of(u)

        for at in range(0, n, blk):
            q = groups(k_ref[u % 3, pl.ds(at, blk), :]) * c1[:, pl.ds(at, win)][None]
            q = q.reshape(blk, win).astype(BF16)
            rhs = jnp.concatenate([right_v[u, pl.ds(at, win), :], tcol[pl.ds(at, win), :]], axis=1)
            o = jnp.dot(q, rhs, preferred_element_type=F32)
            matched = o[:, :chans] * (1.0 / o[:, chans : chans + 1])
            x0[u + REACH, pl.ds(PAD + at, blk), :] = (
                matched - left_v[u, pl.ds(at, blk), :].astype(F32)
            ).astype(BF16)
            rowed = jnp.transpose(o[:, chans:])
            ids = (lax.broadcasted_iota(jnp.int32, (1, blk), 1) + at).astype(F32)
            disp_ref[pl.ds(ln, 1), pl.ds(at, blk)] = ids + (rowed[1:2] + rowed[2:3]) / rowed[0:1]

    def own_step(u, carry):
        load(u, 0).wait()
        load(u, 1).wait()
        partial_lse(u, True)

        @pl.when(has_r)
        def _():
            mt_up(u).start()

        return carry

    lax.fori_loop(0, lines, own_step, 0)
    send_halo(1, 0)

    wload.wait()
    wbig[...] = jnp.zeros(wbig.shape, BF16)
    for k in range(layers):
        for a in range(3):
            tap = a + core * (2 - 2 * a)
            for b in range(3):
                w = w_v[k, tap, b]
                for h in range(2):
                    wbig[k, (a + h) * chans : (a + h + 1) * chans,
                         (3 * h + b) * chans : (3 * h + b + 1) * chans] = w

    def scores_step(u):
        halves = halo_copies(u)
        sends = mt_downs(u)
        per_send = len(halves) // len(sends)
        for i, send in enumerate(sends):
            @pl.when(has_l)
            def _():
                for copy in halves[i * per_send : (i + 1) * per_send]:
                    copy.wait_recv()

            partial_lse(u, False, (i,) if u == last else tuple(range(nblk)))

            @pl.when(has_l)
            def _():
                send.start()

    def send_c2(u):
        row_done(u)

        @pl.when(has_r)
        def _():
            c2_up(u).start()

        @pl.when(has_l)
        def _():
            c2_down(u).start()

    def row_first(u):
        @pl.when(has_l)
        def _():
            mt_up(u).wait_recv()

        row_halo(u)

    def mt_arrived(copies):
        @pl.when(has_r)
        def _():
            for copy in copies:
                copy.wait_recv()

    def row_step(u):
        row_first(u)
        mt_arrived(mt_downs(u))
        row_own(u, 0, nblk)
        row_rows(u, 0, steps)
        send_c2(u)

    def plan_step(u):
        @pl.when(has_l)
        def _():
            c2_up(u).wait_recv()

        @pl.when(has_r)
        def _():
            c2_down(u).wait_recv()

        transport(u)
        for cond, _, copy in line_copies(u):
            @pl.when(cond)
            def _():
                copy.start()

    def wait_slots(slots, edges):
        for _, cond, copy in line_copies(None, slots, edges):
            @pl.when(cond)
            def _():
                copy.wait_recv()

    part = wide // 3 if (wide // 3) % 16 == 0 else wide
    step_rows = 96

    def conv_pair(src, k, slot, store, new_slots=()):
        count = wide // part
        for i in range(count):
            if i == 1 and new_slots:
                wait_slots(new_slots, True)
            g = (i + count // 2) % count
            rows = slice(g * part, (g + 1) * part)
            ins = jnp.concatenate([src[slot - 1 + i, rows, :] for i in range(4)], axis=1)
            y = jnp.dot(ins, wbig[k], preferred_element_type=F32)
            for j in range(6):
                y_ref[j, 8 + g * part : 8 + (g + 1) * part, :] = y[:, j * chans : (j + 1) * chans]
        for h in range(2):
            store(h, src, slot + h, bias_ref[k : k + 1, :])

    def updated(h, src, slot, bias, at, rows):
        total = (
            y_ref[3 * h, 7 + at : 7 + at + rows, :]
            + y_ref[3 * h + 1, 8 + at : 8 + at + rows, :]
            + y_ref[3 * h + 2, 9 + at : 9 + at + rows, :]
        )
        state = src[slot, at : at + rows, :].astype(F32)
        return (state + jnp.maximum(total + bias, 0.0)).astype(BF16)

    def clear_edges(dst, first, last):
        @pl.when(jnp.logical_not(has_l))
        def _():
            dst[first:last, 0:PAD, :] = jnp.zeros((last - first, PAD, chans), BF16)

        @pl.when(jnp.logical_not(has_r))
        def _():
            dst[first:last, n + PAD : wide, :] = jnp.zeros((last - first, PAD, chans), BF16)

        if first < REACH:
            stop = min(last, REACH)

            @pl.when(jnp.logical_not(has_x))
            def _():
                dst[first:stop] = jnp.zeros((stop - first, wide, chans), BF16)

    def layer_pair(src, dst, k, first, new_slots=()):
        wait_slots(new_slots, False)

        def keep(h, src, slot, bias):
            for at in range(0, wide, step_rows):
                dst[slot, at : at + step_rows, :] = updated(h, src, slot, bias, at, step_rows)

        conv_pair(src, k, first, keep, new_slots)
        clear_edges(dst, first, first + 2)

    def line_out(u):
        return pltpu.make_async_copy(out_ref.at[u], out_hbm.at[line_of(u)], out_sem.at[u])

    def put(h, src, slot, bias):
        for at in range(0, n, 128):
            out_ref[slot - REACH, at : at + 128, :] = updated(h, src, slot, bias, at + PAD, 128)
        line_out(slot - REACH).start()

    scores_step(0)
    send_halo(1, 1)
    send_halo(2, 0)
    scores_step(1)
    send_halo(2, 1)
    row_step(0)
    send_halo(3, 0)
    scores_step(2)
    send_halo(3, 1)
    row_step(1)
    plan_step(0)
    scores_step(3)
    row_step(2)
    per = blk // rows_at
    row_first(last)
    mt_arrived(mt_downs(last)[:-1])
    row_own(last, 0, nblk - 1)
    row_rows(last, 0, steps - per)
    mt_arrived(mt_downs(last)[-1:])
    row_own(last, nblk - 1, nblk)
    if per == 1:
        col_sum(last, steps - 1, row_exp(last, steps - 1, row_max(last, steps - 1)))
    else:
        row_rows(last, steps - per, steps)
    send_c2(last)
    plan_step(1)
    plan_step(2)
    plan_step(3)
    disp_out = pltpu.make_async_copy(disp_ref, disp_hbm, out_sem.at[lines])
    disp_out.start()
    layer_pair(x0, x1, 0, 3, (2, 3, 4, 5))
    layer_pair(x0, x1, 0, 1, (0, 1))
    layer_pair(x1, x2, 1, 2)
    layer_pair(x0, x1, 0, 5, (6, 7))
    layer_pair(x0, x1, 0, 7, (8, 9))
    layer_pair(x1, x2, 1, 4)
    layer_pair(x1, x2, 1, 6)
    conv_pair(x2, 2, 3, put)
    conv_pair(x2, 2, 5, put)
    disp_out.wait()
    for u in range(lines):
        line_out(u).wait()

    @pl.when(has_r)
    def _():
        for u in range(lines):
            for copy in halo_copies(u):
                copy.wait_send()
            mt_up(u).wait_send()
            c2_up(u).wait_send()

    @pl.when(has_l)
    def _():
        for u in range(lines):
            for copy in mt_downs(u):
                copy.wait_send()
            c2_down(u).wait_send()

    for cond, _, copy in line_copies(None):
        @pl.when(cond)
        def _():
            copy.wait_send()


def hand_over(pieces, src, disp_src, dst, disp_dst, hold, disp_hold, in_sem, out_sem):
    lines, n, _ = src.shape
    size = lines * n // pieces
    spots = [(k * size // n, pl.ds(k * size % n, size)) for k in range(pieces)]
    loads = [
        pltpu.make_async_copy(src.at[at], hold.at[at], in_sem.at[k]) for k, at in enumerate(spots)
    ]
    stores = [
        pltpu.make_async_copy(hold.at[at], dst.at[at], out_sem.at[k]) for k, at in enumerate(spots)
    ]
    loads.append(pltpu.make_async_copy(disp_src, disp_hold, in_sem.at[pieces]))
    stores.append(pltpu.make_async_copy(disp_hold, disp_dst, out_sem.at[pieces]))
    for load in loads:
        load.start()
    for load, store in zip(loads, stores):
        load.wait()
        store.start()
    for store in stores:
        store.wait()


def shards(segs, line_devs, left, right, weight, bias):
    lines, n, chans = left.shape
    layers = weight.shape[0]
    blk = n // 4
    wide = n + 2 * PAD
    slots = lines + 2 * REACH
    shape = (segs, line_devs, lines, n, blk, chans, layers)
    dma = pltpu.SemaphoreType.DMA
    vm = pltpu.VMEM
    refined, disparity = pl.pallas_call(
        functools.partial(body, shape),
        out_shape=(
            jax.ShapeDtypeStruct((lines, n, chans), BF16),
            jax.ShapeDtypeStruct((lines, n), F32),
        ),
        in_specs=[pl.BlockSpec(memory_space=pl.ANY)] * 3 + [pl.BlockSpec(memory_space=vm)],
        out_specs=(pl.BlockSpec(memory_space=pl.ANY), pl.BlockSpec(memory_space=pl.ANY)),
        scratch_shapes=[
            vm((lines, n, chans), BF16),
            vm((lines, 2 * n, chans), BF16),
            vm((2 * n, chans), BF16),
            vm((lines, n, n + blk), F32),
            vm((3, n, n + blk), F32),
            vm((lines, 2, n), F32),
            vm((lines, 2, n), F32),
            vm((lines, 2, n), F32),
            vm((lines, 2, n), F32),
            vm((8, 2 * n), F32),
            vm((8, 2 * n), F32),
            vm((lines, 1, n), F32),
            vm((lines, 1, n), F32),
            vm((lines, 1, n), F32),
            vm((lines, 1, n), F32),
            vm(weight.shape, BF16),
            vm((layers, 4 * chans, 6 * chans), BF16),
            vm((slots, wide, chans), BF16),
            vm((slots, wide, chans), BF16),
            vm((slots, wide, chans), BF16),
            vm((6, wide + 16, chans), F32),
            dma((lines, 2)),
            dma,
            dma((lines, 4)),
            dma((lines, 4)),
            dma((lines + 4, 2)),
            dma((lines + 4, 2)),
            dma((lines, 2)),
            dma((lines, 2)),
            dma((lines, 3, 3)),
            dma((slots, 3)),
            vm((lines, n, chans), BF16),
            vm((lines, n), F32),
            dma((lines + 1,)),
        ],
        compiler_params=pltpu.CompilerParams(
            collective_id=0, has_side_effects=True, vmem_limit_bytes=60 * 1024 * 1024
        ),
        name="stereo",
    )(left, right, weight, bias)
    pieces = 8
    return pl.pallas_call(
        functools.partial(hand_over, pieces),
        out_shape=(
            jax.ShapeDtypeStruct((lines, n, chans), BF16),
            jax.ShapeDtypeStruct((lines, n), F32),
        ),
        in_specs=[pl.BlockSpec(memory_space=pl.ANY)] * 2,
        out_specs=(pl.BlockSpec(memory_space=pl.ANY), pl.BlockSpec(memory_space=pl.ANY)),
        scratch_shapes=[
            vm((lines, n, chans), BF16),
            vm((lines, n), F32),
            dma((pieces + 1,)),
            dma((pieces + 1,)),
        ],
        name="hand_over",
    )(refined, disparity)


def solution(mesh):
    return jax.shard_map(
        functools.partial(shards, mesh.shape["seg"], mesh.shape["lines"]),
        mesh=mesh,
        in_specs=(P("lines", "seg", None), P("lines", "seg", None), P(), P()),
        out_specs=(P("lines", "seg", None), P("lines", "seg")),
        check_vma=False,
    )
```

```python
import functools
import math

import jax
import jax.numpy as jnp
from jax import lax
from jax.experimental import pallas as pl
from jax.experimental.pallas import tpu as pltpu
from jax.sharding import PartitionSpec as P

NEG = -1e30
LOG2E = 1.4426950408889634
PAD = 16
REACH = 3
MESH = pl.DeviceIdType.MESH
F32 = jnp.float32
BF16 = jnp.bfloat16


def nt_dot(a, b):
    return lax.dot_general(a, b, (((1,), (1,)), ((), ())), preferred_element_type=F32)


def groups(x):
    return x.reshape(x.shape[0] // 8, 8, x.shape[1])


def body(
    shape, left_hbm, right_hbm, w_hbm, bias_ref, out_hbm, disp_hbm,
    left_v, right_v, tcol, s_ref, k_ref, own_mt, halo_mt, own_in, halo_in, c1, c2acc,
    own_c2, halo_c2, own_c2_in, halo_c2_in, w_v, wbig, x0, x1, x2, y_ref,
    load_sem, wsem, halo_ss, halo_rs, mt_ss, mt_rs, c2_ss, c2_rs, ln_ss, ln_rs,
    out_ref, disp_ref, out_sem,
):
    segs, line_devs, lines, n, blk, chans, layers = shape
    nblk = n // blk
    win = n + blk
    wide = n + 2 * PAD
    scale = LOG2E / math.sqrt(chans)
    seg = lax.axis_index("seg")
    me = lax.axis_index("lines")
    core = lax.rem(me, 2)
    mate = me + 1 - 2 * core
    cross = me - 1 + 2 * core
    has_l = seg > 0
    has_r = seg < segs - 1
    has_x = (cross >= 0) & (cross < line_devs)

    def dev(ds, ln):
        return {"seg": seg + ds, "lines": ln}

    def line_of(u):
        return u + core * (lines - 1 - 2 * u)

    def remote(src, dst, ss, rs, where):
        return pltpu.make_async_remote_copy(
            src_ref=src, dst_ref=dst, send_sem=ss, recv_sem=rs, device_id=where, device_id_type=MESH
        )

    barrier = pltpu.get_barrier_semaphore()
    peers = []
    for ds, side in ((-1, has_l), (1, has_r)):
        peers += [(side, dev(ds, me))]
    peers += [(me >= 0, dev(0, mate)), (has_x, dev(0, cross))]
    for cond, where in peers:
        @pl.when(cond)
        def _():
            pl.semaphore_signal(barrier, inc=1, device_id=where, device_id_type=MESH)

    def load(u, which):
        src = (left_hbm, right_hbm)[which].at[line_of(u)]
        dst = left_v.at[u] if which == 0 else right_v.at[u, pl.ds(n, n)]
        return pltpu.make_async_copy(src, dst, load_sem.at[u, which])

    for u in range(lines):
        load(u, 0).start()
        load(u, 1).start()
    wload = pltpu.make_async_copy(w_hbm, w_v, wsem)
    wload.start()

    pl.semaphore_wait(barrier, sum(cond.astype(jnp.int32) for cond, _ in peers))

    last = lines - 1

    def halo_copies(u):
        count = nblk if u == last else 2
        size = n // count
        return [
            remote(
                right_hbm.at[line_of(u), pl.ds(c * size, size)],
                right_v.at[u, pl.ds(c * size, size)],
                halo_ss.at[u, c], halo_rs.at[u, c], dev(1, me),
            )
            for c in range(count)
        ]

    def send_halo(u, half):
        copies = halo_copies(u)
        per_half = len(copies) // 2

        @pl.when(has_r)
        def _():
            for copy in copies[half * per_half : (half + 1) * per_half]:
                copy.start()

    send_halo(0, 0)
    send_halo(0, 1)

    def mt_up(u):
        return remote(own_mt.at[u], halo_in.at[u], mt_ss.at[u, 0], mt_rs.at[u, 0], dev(1, me))

    def mt_down(u, c=None):
        src, dst, sem = halo_mt.at[u], own_in.at[u], u
        if c is not None:
            cols = pl.ds(c * blk, blk)
            src, dst, sem = halo_mt.at[u, :, cols], own_in.at[u, :, cols], lines + c
        return remote(src, dst, mt_ss.at[sem, 1], mt_rs.at[sem, 1], dev(-1, me))

    def mt_downs(u):
        return [mt_down(u, c) for c in range(nblk)] if u == last else [mt_down(u)]

    def c2_up(u):
        return remote(own_c2.at[u], halo_c2_in.at[u], c2_ss.at[u, 0], c2_rs.at[u, 0], dev(1, me))

    def c2_down(u):
        return remote(halo_c2.at[u], own_c2_in.at[u], c2_ss.at[u, 1], c2_rs.at[u, 1], dev(-1, me))

    def line_routes():
        routes = []
        for u in range(lines):
            routes.append((u, u + REACH, None, 0, me))
            if u < REACH:
                routes.append((u, REACH - 1 - u, has_x, 1, cross))
            if u >= lines - REACH:
                routes.append((u, 2 * lines + REACH - 1 - u, None, 2, mate))
        return routes

    def line_copies(u_pick, slots=None, edges=None):
        copies = []
        for u, slot, cond, to, ln in line_routes():
            if u_pick is not None and u != u_pick or slots is not None and slot not in slots:
                continue
            mine = u + REACH
            cond = me >= 0 if cond is None else cond
            if to and edges is not True:
                copies.append((cond, cond, remote(
                    x0.at[mine, pl.ds(PAD, n)], x0.at[slot, pl.ds(PAD, n)],
                    ln_ss.at[u, to, 0], ln_rs.at[slot, 0], dev(0, ln))))
            if edges is False:
                continue
            copies.append((cond & has_r, cond & has_l, remote(
                x0.at[mine, pl.ds(n, PAD)], x0.at[slot, pl.ds(0, PAD)],
                ln_ss.at[u, to, 1], ln_rs.at[slot, 1], dev(1, ln))))
            copies.append((cond & has_l, cond & has_r, remote(
                x0.at[mine, pl.ds(PAD, PAD)], x0.at[slot, pl.ds(n + PAD, PAD)],
                ln_ss.at[u, to, 2], ln_rs.at[slot, 2], dev(-1, ln))))
        return copies

    e_ids = lax.broadcasted_iota(jnp.int32, (2 * n, chans), 0)
    lane = lax.broadcasted_iota(jnp.int32, (2 * n, chans), 1)
    t = n - e_ids
    low = t & 7
    tcol[...] = jnp.where(
        lane == 0, 1, jnp.where(lane == 1, t - low, jnp.where(lane == 2, low, 0))
    ).astype(F32).astype(BF16)

    @pl.when(jnp.logical_not(has_l))
    def _():
        right_v[:, 0:n, :] = jnp.zeros((lines, n, chans), BF16)
        halo_in[:, 0:1, :] = jnp.full((lines, 1, n), NEG, F32)
        halo_in[:, 1:2, :] = jnp.zeros((lines, 1, n), F32)
        halo_c2_in[...] = jnp.zeros((lines, 1, n), F32)
        x0[:, 0:PAD, :] = jnp.zeros((lines + 2 * REACH, PAD, chans), BF16)

    @pl.when(jnp.logical_not(has_r))
    def _():
        own_in[:, 0:1, :] = jnp.full((lines, 1, n), NEG, F32)
        own_in[:, 1:2, :] = jnp.zeros((lines, 1, n), F32)
        own_c2_in[...] = jnp.zeros((lines, 1, n), F32)
        x0[:, n + PAD : wide, :] = jnp.zeros((lines + 2 * REACH, PAD, chans), BF16)

    @pl.when(jnp.logical_not(has_x))
    def _():
        x0[0:REACH] = jnp.zeros((REACH, wide, chans), BF16)

    y_ref[:, 0:8, :] = jnp.zeros((6, 8, chans), F32)
    y_ref[:, 8 + wide : 16 + wide, :] = jnp.zeros((6, 8, chans), F32)

    il = lax.broadcasted_iota(jnp.int32, (blk // 2, blk), 0)
    jl = lax.broadcasted_iota(jnp.int32, (blk // 2, blk), 1)

    def partial_lse(u, own, chunks=tuple(range(nblk))):
        base = n if own else 0
        dst = own_mt if own else halo_mt
        for c in chunks:
            cols = right_v[u, base + c * blk : base + (c + 1) * blk, :]
            pieces = []
            top = jnp.full((8, blk), NEG, F32)
            for r in range(c, nblk) if own else range(c + 1):
                at = base + (c - r) * blk
                for h in range(2):
                    rows = slice(r * blk + h * (blk // 2), r * blk + (h + 1) * (blk // 2))
                    s = nt_dot(left_v[u, rows, :], cols) * scale
                    if r == c:
                        ih = il + h * (blk // 2)
                        s = jnp.where(jl <= ih if own else jl > ih, s, NEG)
                    s_ref[u, rows, at : at + blk] = s
                    top = jnp.maximum(top, jnp.max(groups(s), axis=0))
                    pieces.append((rows, at))
            total = jnp.zeros((8, blk), F32)
            for rows, at in pieces:
                g = groups(s_ref[u, rows, at : at + blk])
                total = total + jnp.sum(jnp.exp2(g - top[None]), axis=0)
            m = jnp.max(top, axis=0, keepdims=True)
            dst[u, 0:1, c * blk : (c + 1) * blk] = m
            dst[u, 1:2, c * blk : (c + 1) * blk] = jnp.sum(
                total * jnp.exp2(top - m), axis=0, keepdims=True
            )

    def col_pot(a, b):
        m = jnp.maximum(a[0:1], b[0:1])
        tot = a[1:2] * jnp.exp2(a[0:1] - m) + b[1:2] * jnp.exp2(b[0:1] - m)
        return -(m + jnp.log(tot) * LOG2E)

    rows_at = min(128, blk)
    steps = n // rows_at
    tiles = [slice(j * 128, min(win, (j + 1) * 128)) for j in range(-(-win // 128))]

    def pot_at(k):
        return pl.multiple_of((k * rows_at) // blk * blk, blk)

    def row_max(u, k):
        here = pl.ds(pl.multiple_of(k * rows_at, rows_at), rows_at)
        top = None
        for tile in tiles:
            width = tile.stop - tile.start
            pot = c1[:, pl.ds(pot_at(k) + tile.start, width)]
            t = groups(s_ref[u, here, tile]) + pot[None]
            if width < 128:
                t = jnp.concatenate([t] * (128 // width), axis=2)
            top = t if top is None else jnp.maximum(top, t)
        return jnp.broadcast_to(jnp.max(top, axis=2, keepdims=True), top.shape)

    def row_exp(u, k, top):
        here = pl.ds(pl.multiple_of(k * rows_at, rows_at), rows_at)
        total = None
        for tile in tiles:
            width = tile.stop - tile.start
            pot = c1[:, pl.ds(pot_at(k) + tile.start, width)]
            t = groups(s_ref[u, here, tile]) + pot[None]
            e = jnp.exp2(t - top[:, :, :width])
            k_ref[u % 3, here, tile] = e.reshape(rows_at, width)
            if width < 128:
                e = jnp.concatenate([e, jnp.zeros(e.shape[:2] + (128 - width,), F32)], axis=2)
            total = e if total is None else total + e
        return jnp.broadcast_to(1.0 / jnp.sum(total, axis=2, keepdims=True), total.shape)

    def col_sum(u, k, inv):
        here = pl.ds(pl.multiple_of(k * rows_at, rows_at), rows_at)
        for tile in tiles:
            width = tile.stop - tile.start
            part = jnp.sum(groups(k_ref[u % 3, here, tile]) * inv[:, :, :width], axis=0)
            c2acc[:, pl.ds(pot_at(k) + tile.start, width)] += part

    def row_halo(u):
        halo = jnp.where(has_l, col_pot(halo_mt[u], halo_in[u]), NEG)
        c1[:, 0:n] = jnp.broadcast_to(halo, (8, n))
        c2acc[...] = jnp.zeros((8, 2 * n), F32)

    def row_own(u, c0, c1_):
        cols = slice(c0 * blk, c1_ * blk)
        own = col_pot(own_mt[u, :, cols], own_in[u, :, cols])
        c1[:, n + c0 * blk : n + c1_ * blk] = jnp.broadcast_to(own, (8, (c1_ - c0) * blk))

    def row_rows(u, first, stop):
        inv = row_exp(u, first, row_max(u, first))
        top = row_max(u, first + 1)

        def step(k, carry):
            top, inv = carry
            col_sum(u, k - 2, inv)
            inv = row_exp(u, k - 1, top)
            return row_max(u, k), inv

        if stop > first + 2:
            top, inv = lax.fori_loop(first + 2, stop, step, (top, inv))
        col_sum(u, stop - 2, inv)
        col_sum(u, stop - 1, row_exp(u, stop - 1, top))

    def row_done(u):
        halo_c2[u] = jnp.sum(c2acc[:, 0:n], axis=0, keepdims=True)
        own_c2[u] = jnp.sum(c2acc[:, n : 2 * n], axis=0, keepdims=True)

    def transport(u):
        c1[:, n : 2 * n] = jnp.broadcast_to(1.0 / (own_c2[u] + own_c2_in[u]), (8, n))
        c1[:, 0:n] = jnp.broadcast_to(
            jnp.where(has_l, 1.0 / (halo_c2[u] + halo_c2_in[u]), 0.0), (8, n)
        )
        ln = line_of(u)

        for at in range(0, n, blk):
            q = groups(k_ref[u % 3, pl.ds(at, blk), :]) * c1[:, pl.ds(at, win)][None]
            q = q.reshape(blk, win).astype(BF16)
            rhs = jnp.concatenate([right_v[u, pl.ds(at, win), :], tcol[pl.ds(at, win), :]], axis=1)
            o = jnp.dot(q, rhs, preferred_element_type=F32)
            matched = o[:, :chans] * (1.0 / o[:, chans : chans + 1])
            x0[u + REACH, pl.ds(PAD + at, blk), :] = (
                matched - left_v[u, pl.ds(at, blk), :].astype(F32)
            ).astype(BF16)
            rowed = jnp.transpose(o[:, chans:])
            ids = (lax.broadcasted_iota(jnp.int32, (1, blk), 1) + at).astype(F32)
            disp_ref[pl.ds(ln, 1), pl.ds(at, blk)] = ids + (rowed[1:2] + rowed[2:3]) / rowed[0:1]

    def own_step(u, carry):
        load(u, 0).wait()
        load(u, 1).wait()
        partial_lse(u, True)

        @pl.when(has_r)
        def _():
            mt_up(u).start()

        return carry

    lax.fori_loop(0, lines, own_step, 0)
    send_halo(1, 0)

    wload.wait()
    wbig[...] = jnp.zeros(wbig.shape, BF16)
    for k in range(layers):
        for a in range(3):
            tap = a + core * (2 - 2 * a)
            for b in range(3):
                w = w_v[k, tap, b]
                for h in range(2):
                    wbig[k, (a + h) * chans : (a + h + 1) * chans,
                         (3 * h + b) * chans : (3 * h + b + 1) * chans] = w

    def scores_step(u):
        halves = halo_copies(u)
        sends = mt_downs(u)
        per_send = len(halves) // len(sends)
        for i, send in enumerate(sends):
            @pl.when(has_l)
            def _():
                for copy in halves[i * per_send : (i + 1) * per_send]:
                    copy.wait_recv()

            partial_lse(u, False, (i,) if u == last else tuple(range(nblk)))

            @pl.when(has_l)
            def _():
                send.start()

    def send_c2(u):
        row_done(u)

        @pl.when(has_r)
        def _():
            c2_up(u).start()

        @pl.when(has_l)
        def _():
            c2_down(u).start()

    def row_first(u):
        @pl.when(has_l)
        def _():
            mt_up(u).wait_recv()

        row_halo(u)

    def mt_arrived(copies):
        @pl.when(has_r)
        def _():
            for copy in copies:
                copy.wait_recv()

    def row_step(u):
        row_first(u)
        mt_arrived(mt_downs(u))
        row_own(u, 0, nblk)
        row_rows(u, 0, steps)
        send_c2(u)

    def plan_step(u):
        @pl.when(has_l)
        def _():
            c2_up(u).wait_recv()

        @pl.when(has_r)
        def _():
            c2_down(u).wait_recv()

        transport(u)
        for cond, _, copy in line_copies(u):
            @pl.when(cond)
            def _():
                copy.start()

    def wait_slots(slots, edges):
        for _, cond, copy in line_copies(None, slots, edges):
            @pl.when(cond)
            def _():
                copy.wait_recv()

    part = wide // 3 if (wide // 3) % 16 == 0 else wide
    step_rows = 96

    def conv_pair(src, k, slot, store, new_slots=()):
        count = wide // part
        for i in range(count):
            if i == 1 and new_slots:
                wait_slots(new_slots, True)
            g = (i + count // 2) % count
            rows = slice(g * part, (g + 1) * part)
            ins = jnp.concatenate([src[slot - 1 + i, rows, :] for i in range(4)], axis=1)
            y = jnp.dot(ins, wbig[k], preferred_element_type=F32)
            for j in range(6):
                y_ref[j, 8 + g * part : 8 + (g + 1) * part, :] = y[:, j * chans : (j + 1) * chans]
        for h in range(2):
            store(h, src, slot + h, bias_ref[k : k + 1, :])

    def updated(h, src, slot, bias, at, rows):
        total = (
            y_ref[3 * h, 7 + at : 7 + at + rows, :]
            + y_ref[3 * h + 1, 8 + at : 8 + at + rows, :]
            + y_ref[3 * h + 2, 9 + at : 9 + at + rows, :]
        )
        state = src[slot, at : at + rows, :].astype(F32)
        return (state + jnp.maximum(total + bias, 0.0)).astype(BF16)

    def clear_edges(dst, first, last):
        @pl.when(jnp.logical_not(has_l))
        def _():
            dst[first:last, 0:PAD, :] = jnp.zeros((last - first, PAD, chans), BF16)

        @pl.when(jnp.logical_not(has_r))
        def _():
            dst[first:last, n + PAD : wide, :] = jnp.zeros((last - first, PAD, chans), BF16)

        if first < REACH:
            stop = min(last, REACH)

            @pl.when(jnp.logical_not(has_x))
            def _():
                dst[first:stop] = jnp.zeros((stop - first, wide, chans), BF16)

    def layer_pair(src, dst, k, first, new_slots=()):
        wait_slots(new_slots, False)

        def keep(h, src, slot, bias):
            for at in range(0, wide, step_rows):
                dst[slot, at : at + step_rows, :] = updated(h, src, slot, bias, at, step_rows)

        conv_pair(src, k, first, keep, new_slots)
        clear_edges(dst, first, first + 2)

    def line_out(u):
        return pltpu.make_async_copy(out_ref.at[u], out_hbm.at[line_of(u)], out_sem.at[u])

    def put(h, src, slot, bias):
        for at in range(0, n, 128):
            out_ref[slot - REACH, at : at + 128, :] = updated(h, src, slot, bias, at + PAD, 128)
        line_out(slot - REACH).start()

    scores_step(0)
    send_halo(1, 1)
    send_halo(2, 0)
    scores_step(1)
    send_halo(2, 1)
    row_step(0)
    send_halo(3, 0)
    scores_step(2)
    send_halo(3, 1)
    row_step(1)
    plan_step(0)
    scores_step(3)
    row_step(2)
    plan_step(1)
    per = blk // rows_at
    row_first(last)
    mt_arrived(mt_downs(last)[:-1])
    row_own(last, 0, nblk - 1)
    row_rows(last, 0, steps - per)
    mt_arrived(mt_downs(last)[-1:])
    row_own(last, nblk - 1, nblk)
    if per == 1:
        col_sum(last, steps - 1, row_exp(last, steps - 1, row_max(last, steps - 1)))
    else:
        row_rows(last, steps - per, steps)
    send_c2(last)
    plan_step(2)
    plan_step(3)
    disp_out = pltpu.make_async_copy(disp_ref, disp_hbm, out_sem.at[lines])
    disp_out.start()
    layer_pair(x0, x1, 0, 3, (2, 3, 4, 5))
    layer_pair(x0, x1, 0, 1, (0, 1))
    layer_pair(x1, x2, 1, 2)
    layer_pair(x0, x1, 0, 5, (6, 7))
    layer_pair(x0, x1, 0, 7, (8, 9))
    layer_pair(x1, x2, 1, 4)
    layer_pair(x1, x2, 1, 6)
    conv_pair(x2, 2, 3, put)
    conv_pair(x2, 2, 5, put)
    disp_out.wait()
    for u in range(lines):
        line_out(u).wait()

    @pl.when(has_r)
    def _():
        for u in range(lines):
            for copy in halo_copies(u):
                copy.wait_send()
            mt_up(u).wait_send()
            c2_up(u).wait_send()

    @pl.when(has_l)
    def _():
        for u in range(lines):
            for copy in mt_downs(u):
                copy.wait_send()
            c2_down(u).wait_send()

    for cond, _, copy in line_copies(None):
        @pl.when(cond)
        def _():
            copy.wait_send()


def hand_over(pieces, src, disp_src, dst, disp_dst, hold, disp_hold, in_sem, out_sem):
    lines, n, _ = src.shape
    size = lines * n // pieces
    spots = [(k * size // n, pl.ds(k * size % n, size)) for k in range(pieces)]
    loads = [
        pltpu.make_async_copy(src.at[at], hold.at[at], in_sem.at[k]) for k, at in enumerate(spots)
    ]
    stores = [
        pltpu.make_async_copy(hold.at[at], dst.at[at], out_sem.at[k]) for k, at in enumerate(spots)
    ]
    loads.append(pltpu.make_async_copy(disp_src, disp_hold, in_sem.at[pieces]))
    stores.append(pltpu.make_async_copy(disp_hold, disp_dst, out_sem.at[pieces]))
    for load in loads:
        load.start()
    for load, store in zip(loads, stores):
        load.wait()
        store.start()
    for store in stores:
        store.wait()


def shards(segs, line_devs, left, right, weight, bias):
    lines, n, chans = left.shape
    layers = weight.shape[0]
    blk = n // 4
    wide = n + 2 * PAD
    slots = lines + 2 * REACH
    shape = (segs, line_devs, lines, n, blk, chans, layers)
    dma = pltpu.SemaphoreType.DMA
    vm = pltpu.VMEM
    refined, disparity = pl.pallas_call(
        functools.partial(body, shape),
        out_shape=(
            jax.ShapeDtypeStruct((lines, n, chans), BF16),
            jax.ShapeDtypeStruct((lines, n), F32),
        ),
        in_specs=[pl.BlockSpec(memory_space=pl.ANY)] * 3 + [pl.BlockSpec(memory_space=vm)],
        out_specs=(pl.BlockSpec(memory_space=pl.ANY), pl.BlockSpec(memory_space=pl.ANY)),
        scratch_shapes=[
            vm((lines, n, chans), BF16),
            vm((lines, 2 * n, chans), BF16),
            vm((2 * n, chans), BF16),
            vm((lines, n, n + blk), F32),
            vm((3, n, n + blk), F32),
            vm((lines, 2, n), F32),
            vm((lines, 2, n), F32),
            vm((lines, 2, n), F32),
            vm((lines, 2, n), F32),
            vm((8, 2 * n), F32),
            vm((8, 2 * n), F32),
            vm((lines, 1, n), F32),
            vm((lines, 1, n), F32),
            vm((lines, 1, n), F32),
            vm((lines, 1, n), F32),
            vm(weight.shape, BF16),
            vm((layers, 4 * chans, 6 * chans), BF16),
            vm((slots, wide, chans), BF16),
            vm((slots, wide, chans), BF16),
            vm((slots, wide, chans), BF16),
            vm((6, wide + 16, chans), F32),
            dma((lines, 2)),
            dma,
            dma((lines, 4)),
            dma((lines, 4)),
            dma((lines + 4, 2)),
            dma((lines + 4, 2)),
            dma((lines, 2)),
            dma((lines, 2)),
            dma((lines, 3, 3)),
            dma((slots, 3)),
            vm((lines, n, chans), BF16),
            vm((lines, n), F32),
            dma((lines + 1,)),
        ],
        compiler_params=pltpu.CompilerParams(
            collective_id=0, has_side_effects=True, vmem_limit_bytes=60 * 1024 * 1024
        ),
        name="stereo",
    )(left, right, weight, bias)
    pieces = 8
    return pl.pallas_call(
        functools.partial(hand_over, pieces),
        out_shape=(
            jax.ShapeDtypeStruct((lines, n, chans), BF16),
            jax.ShapeDtypeStruct((lines, n), F32),
        ),
        in_specs=[pl.BlockSpec(memory_space=pl.ANY)] * 2,
        out_specs=(pl.BlockSpec(memory_space=pl.ANY), pl.BlockSpec(memory_space=pl.ANY)),
        scratch_shapes=[
            vm((lines, n, chans), BF16),
            vm((lines, n), F32),
            dma((pieces + 1,)),
            dma((pieces + 1,)),
        ],
        name="hand_over",
    )(refined, disparity)


def solution(mesh):
    return jax.shard_map(
        functools.partial(shards, mesh.shape["seg"], mesh.shape["lines"]),
        mesh=mesh,
        in_specs=(P("lines", "seg", None), P("lines", "seg", None), P(), P()),
        out_specs=(P("lines", "seg", None), P("lines", "seg")),
        check_vma=False,
    )
```

```python
import functools
import math

import jax
import jax.numpy as jnp
from jax import lax
from jax.experimental import pallas as pl
from jax.experimental.pallas import tpu as pltpu
from jax.sharding import PartitionSpec as P

NEG = -1e30
LOG2E = 1.4426950408889634
PAD = 16
REACH = 3
MESH = pl.DeviceIdType.MESH
F32 = jnp.float32
BF16 = jnp.bfloat16


def nt_dot(a, b):
    return lax.dot_general(a, b, (((1,), (1,)), ((), ())), preferred_element_type=F32)


def groups(x):
    return x.reshape(x.shape[0] // 8, 8, x.shape[1])


def body(
    shape, left_hbm, right_hbm, w_hbm, bias_ref, out_hbm, disp_hbm,
    left_v, right_v, tcol, s_ref, k_ref, own_mt, halo_mt, own_in, halo_in, c1, c2acc,
    own_c2, halo_c2, own_c2_in, halo_c2_in, w_v, wbig, x0, x1, x2, y_ref,
    load_sem, wsem, halo_ss, halo_rs, mt_ss, mt_rs, c2_ss, c2_rs, ln_ss, ln_rs,
    out_ref, disp_ref, out_sem,
):
    segs, line_devs, lines, n, blk, chans, layers = shape
    nblk = n // blk
    win = n + blk
    wide = n + 2 * PAD
    scale = LOG2E / math.sqrt(chans)
    seg = lax.axis_index("seg")
    me = lax.axis_index("lines")
    core = lax.rem(me, 2)
    mate = me + 1 - 2 * core
    cross = me - 1 + 2 * core
    has_l = seg > 0
    has_r = seg < segs - 1
    has_x = (cross >= 0) & (cross < line_devs)

    def dev(ds, ln):
        return {"seg": seg + ds, "lines": ln}

    def line_of(u):
        return u + core * (lines - 1 - 2 * u)

    def remote(src, dst, ss, rs, where):
        return pltpu.make_async_remote_copy(
            src_ref=src, dst_ref=dst, send_sem=ss, recv_sem=rs, device_id=where, device_id_type=MESH
        )

    barrier = pltpu.get_barrier_semaphore()
    peers = []
    for ds, side in ((-1, has_l), (1, has_r)):
        peers += [(side, dev(ds, me))]
    peers += [(me >= 0, dev(0, mate)), (has_x, dev(0, cross))]
    for cond, where in peers:
        @pl.when(cond)
        def _():
            pl.semaphore_signal(barrier, inc=1, device_id=where, device_id_type=MESH)

    def load(u, which):
        src = (left_hbm, right_hbm)[which].at[line_of(u)]
        dst = left_v.at[u] if which == 0 else right_v.at[u, pl.ds(n, n)]
        return pltpu.make_async_copy(src, dst, load_sem.at[u, which])

    for u in range(lines):
        load(u, 0).start()
        load(u, 1).start()
    wload = pltpu.make_async_copy(w_hbm, w_v, wsem)
    wload.start()

    pl.semaphore_wait(barrier, sum(cond.astype(jnp.int32) for cond, _ in peers))

    last = lines - 1

    def halo_copies(u):
        count = nblk if u == last else 2
        size = n // count
        return [
            remote(
                right_hbm.at[line_of(u), pl.ds(c * size, size)],
                right_v.at[u, pl.ds(c * size, size)],
                halo_ss.at[u, c], halo_rs.at[u, c], dev(1, me),
            )
            for c in range(count)
        ]

    def send_halo(u, half):
        copies = halo_copies(u)
        per_half = len(copies) // 2

        @pl.when(has_r)
        def _():
            for copy in copies[half * per_half : (half + 1) * per_half]:
                copy.start()

    send_halo(0, 0)
    send_halo(0, 1)
    send_halo(1, 0)

    def mt_up(u):
        return remote(own_mt.at[u], halo_in.at[u], mt_ss.at[u, 0], mt_rs.at[u, 0], dev(1, me))

    def mt_down(u, c=None):
        src, dst, sem = halo_mt.at[u], own_in.at[u], u
        if c is not None:
            cols = pl.ds(c * blk, blk)
            src, dst, sem = halo_mt.at[u, :, cols], own_in.at[u, :, cols], lines + c
        return remote(src, dst, mt_ss.at[sem, 1], mt_rs.at[sem, 1], dev(-1, me))

    def mt_downs(u):
        return [mt_down(u, c) for c in range(nblk)] if u == last else [mt_down(u)]

    def c2_up(u):
        return remote(own_c2.at[u], halo_c2_in.at[u], c2_ss.at[u, 0], c2_rs.at[u, 0], dev(1, me))

    def c2_down(u):
        return remote(halo_c2.at[u], own_c2_in.at[u], c2_ss.at[u, 1], c2_rs.at[u, 1], dev(-1, me))

    def line_routes():
        routes = []
        for u in range(lines):
            routes.append((u, u + REACH, None, 0, me))
            if u < REACH:
                routes.append((u, REACH - 1 - u, has_x, 1, cross))
            if u >= lines - REACH:
                routes.append((u, 2 * lines + REACH - 1 - u, None, 2, mate))
        return routes

    def line_copies(u_pick, slots=None, edges=None):
        copies = []
        for u, slot, cond, to, ln in line_routes():
            if u_pick is not None and u != u_pick or slots is not None and slot not in slots:
                continue
            mine = u + REACH
            cond = me >= 0 if cond is None else cond
            if to and edges is not True:
                copies.append((cond, cond, remote(
                    x0.at[mine, pl.ds(PAD, n)], x0.at[slot, pl.ds(PAD, n)],
                    ln_ss.at[u, to, 0], ln_rs.at[slot, 0], dev(0, ln))))
            if edges is False:
                continue
            copies.append((cond & has_r, cond & has_l, remote(
                x0.at[mine, pl.ds(n, PAD)], x0.at[slot, pl.ds(0, PAD)],
                ln_ss.at[u, to, 1], ln_rs.at[slot, 1], dev(1, ln))))
            copies.append((cond & has_l, cond & has_r, remote(
                x0.at[mine, pl.ds(PAD, PAD)], x0.at[slot, pl.ds(n + PAD, PAD)],
                ln_ss.at[u, to, 2], ln_rs.at[slot, 2], dev(-1, ln))))
        return copies

    e_ids = lax.broadcasted_iota(jnp.int32, (2 * n, chans), 0)
    lane = lax.broadcasted_iota(jnp.int32, (2 * n, chans), 1)
    t = n - e_ids
    low = t & 7
    tcol[...] = jnp.where(
        lane == 0, 1, jnp.where(lane == 1, t - low, jnp.where(lane == 2, low, 0))
    ).astype(F32).astype(BF16)

    @pl.when(jnp.logical_not(has_l))
    def _():
        right_v[:, 0:n, :] = jnp.zeros((lines, n, chans), BF16)
        halo_in[:, 0:1, :] = jnp.full((lines, 1, n), NEG, F32)
        halo_in[:, 1:2, :] = jnp.zeros((lines, 1, n), F32)
        halo_c2_in[...] = jnp.zeros((lines, 1, n), F32)
        x0[:, 0:PAD, :] = jnp.zeros((lines + 2 * REACH, PAD, chans), BF16)

    @pl.when(jnp.logical_not(has_r))
    def _():
        own_in[:, 0:1, :] = jnp.full((lines, 1, n), NEG, F32)
        own_in[:, 1:2, :] = jnp.zeros((lines, 1, n), F32)
        own_c2_in[...] = jnp.zeros((lines, 1, n), F32)
        x0[:, n + PAD : wide, :] = jnp.zeros((lines + 2 * REACH, PAD, chans), BF16)

    @pl.when(jnp.logical_not(has_x))
    def _():
        x0[0:REACH] = jnp.zeros((REACH, wide, chans), BF16)

    y_ref[:, 0:8, :] = jnp.zeros((6, 8, chans), F32)
    y_ref[:, 8 + wide : 16 + wide, :] = jnp.zeros((6, 8, chans), F32)

    il = lax.broadcasted_iota(jnp.int32, (blk // 2, blk), 0)
    jl = lax.broadcasted_iota(jnp.int32, (blk // 2, blk), 1)

    def partial_lse(u, own, chunks=tuple(range(nblk))):
        base = n if own else 0
        dst = own_mt if own else halo_mt
        for c in chunks:
            cols = right_v[u, base + c * blk : base + (c + 1) * blk, :]
            pieces = []
            top = jnp.full((8, blk), NEG, F32)
            for r in range(c, nblk) if own else range(c + 1):
                at = base + (c - r) * blk
                for h in range(2):
                    rows = slice(r * blk + h * (blk // 2), r * blk + (h + 1) * (blk // 2))
                    s = nt_dot(left_v[u, rows, :], cols) * scale
                    if r == c:
                        ih = il + h * (blk // 2)
                        s = jnp.where(jl <= ih if own else jl > ih, s, NEG)
                    s_ref[u, rows, at : at + blk] = s
                    top = jnp.maximum(top, jnp.max(groups(s), axis=0))
                    pieces.append((rows, at))
            total = jnp.zeros((8, blk), F32)
            for rows, at in pieces:
                g = groups(s_ref[u, rows, at : at + blk])
                total = total + jnp.sum(jnp.exp2(g - top[None]), axis=0)
            m = jnp.max(top, axis=0, keepdims=True)
            dst[u, 0:1, c * blk : (c + 1) * blk] = m
            dst[u, 1:2, c * blk : (c + 1) * blk] = jnp.sum(
                total * jnp.exp2(top - m), axis=0, keepdims=True
            )

    def col_pot(a, b):
        m = jnp.maximum(a[0:1], b[0:1])
        tot = a[1:2] * jnp.exp2(a[0:1] - m) + b[1:2] * jnp.exp2(b[0:1] - m)
        return -(m + jnp.log(tot) * LOG2E)

    rows_at = min(128, blk)
    steps = n // rows_at
    tiles = [slice(j * 128, min(win, (j + 1) * 128)) for j in range(-(-win // 128))]

    def pot_at(k):
        return pl.multiple_of((k * rows_at) // blk * blk, blk)

    def row_max(u, k):
        here = pl.ds(pl.multiple_of(k * rows_at, rows_at), rows_at)
        top = None
        for tile in tiles:
            width = tile.stop - tile.start
            pot = c1[:, pl.ds(pot_at(k) + tile.start, width)]
            t = groups(s_ref[u, here, tile]) + pot[None]
            if width < 128:
                t = jnp.concatenate([t] * (128 // width), axis=2)
            top = t if top is None else jnp.maximum(top, t)
        return jnp.broadcast_to(jnp.max(top, axis=2, keepdims=True), top.shape)

    def row_exp(u, k, top):
        here = pl.ds(pl.multiple_of(k * rows_at, rows_at), rows_at)
        total = None
        for tile in tiles:
            width = tile.stop - tile.start
            pot = c1[:, pl.ds(pot_at(k) + tile.start, width)]
            t = groups(s_ref[u, here, tile]) + pot[None]
            e = jnp.exp2(t - top[:, :, :width])
            k_ref[u % 3, here, tile] = e.reshape(rows_at, width)
            if width < 128:
                e = jnp.concatenate([e, jnp.zeros(e.shape[:2] + (128 - width,), F32)], axis=2)
            total = e if total is None else total + e
        return jnp.broadcast_to(1.0 / jnp.sum(total, axis=2, keepdims=True), total.shape)

    def col_sum(u, k, inv):
        here = pl.ds(pl.multiple_of(k * rows_at, rows_at), rows_at)
        for tile in tiles:
            width = tile.stop - tile.start
            part = jnp.sum(groups(k_ref[u % 3, here, tile]) * inv[:, :, :width], axis=0)
            c2acc[:, pl.ds(pot_at(k) + tile.start, width)] += part

    def row_halo(u):
        halo = jnp.where(has_l, col_pot(halo_mt[u], halo_in[u]), NEG)
        c1[:, 0:n] = jnp.broadcast_to(halo, (8, n))
        c2acc[...] = jnp.zeros((8, 2 * n), F32)

    def row_own(u, c0, c1_):
        cols = slice(c0 * blk, c1_ * blk)
        own = col_pot(own_mt[u, :, cols], own_in[u, :, cols])
        c1[:, n + c0 * blk : n + c1_ * blk] = jnp.broadcast_to(own, (8, (c1_ - c0) * blk))

    def row_rows(u, first, stop):
        inv = row_exp(u, first, row_max(u, first))
        top = row_max(u, first + 1)

        def step(k, carry):
            top, inv = carry
            col_sum(u, k - 2, inv)
            inv = row_exp(u, k - 1, top)
            return row_max(u, k), inv

        if stop > first + 2:
            top, inv = lax.fori_loop(first + 2, stop, step, (top, inv))
        col_sum(u, stop - 2, inv)
        col_sum(u, stop - 1, row_exp(u, stop - 1, top))

    def row_done(u):
        halo_c2[u] = jnp.sum(c2acc[:, 0:n], axis=0, keepdims=True)
        own_c2[u] = jnp.sum(c2acc[:, n : 2 * n], axis=0, keepdims=True)

    def transport(u):
        c1[:, n : 2 * n] = jnp.broadcast_to(1.0 / (own_c2[u] + own_c2_in[u]), (8, n))
        c1[:, 0:n] = jnp.broadcast_to(
            jnp.where(has_l, 1.0 / (halo_c2[u] + halo_c2_in[u]), 0.0), (8, n)
        )
        ln = line_of(u)

        for at in range(0, n, blk):
            q = groups(k_ref[u % 3, pl.ds(at, blk), :]) * c1[:, pl.ds(at, win)][None]
            q = q.reshape(blk, win).astype(BF16)
            rhs = jnp.concatenate([right_v[u, pl.ds(at, win), :], tcol[pl.ds(at, win), :]], axis=1)
            o = jnp.dot(q, rhs, preferred_element_type=F32)
            matched = o[:, :chans] * (1.0 / o[:, chans : chans + 1])
            x0[u + REACH, pl.ds(PAD + at, blk), :] = (
                matched - left_v[u, pl.ds(at, blk), :].astype(F32)
            ).astype(BF16)
            rowed = jnp.transpose(o[:, chans:])
            ids = (lax.broadcasted_iota(jnp.int32, (1, blk), 1) + at).astype(F32)
            disp_ref[pl.ds(ln, 1), pl.ds(at, blk)] = ids + (rowed[1:2] + rowed[2:3]) / rowed[0:1]

    def own_step(u, carry):
        load(u, 0).wait()
        load(u, 1).wait()
        partial_lse(u, True)

        @pl.when(has_r)
        def _():
            mt_up(u).start()

        return carry

    lax.fori_loop(0, lines, own_step, 0)

    wload.wait()
    wbig[...] = jnp.zeros(wbig.shape, BF16)
    for k in range(layers):
        for a in range(3):
            tap = a + core * (2 - 2 * a)
            for b in range(3):
                w = w_v[k, tap, b]
                for h in range(2):
                    wbig[k, (a + h) * chans : (a + h + 1) * chans,
                         (3 * h + b) * chans : (3 * h + b + 1) * chans] = w

    def scores_step(u):
        halves = halo_copies(u)
        sends = mt_downs(u)
        per_send = len(halves) // len(sends)
        for i, send in enumerate(sends):
            @pl.when(has_l)
            def _():
                for copy in halves[i * per_send : (i + 1) * per_send]:
                    copy.wait_recv()

            partial_lse(u, False, (i,) if u == last else tuple(range(nblk)))

            @pl.when(has_l)
            def _():
                send.start()

    def send_c2(u):
        row_done(u)

        @pl.when(has_r)
        def _():
            c2_up(u).start()

        @pl.when(has_l)
        def _():
            c2_down(u).start()

    def row_first(u):
        @pl.when(has_l)
        def _():
            mt_up(u).wait_recv()

        row_halo(u)

    def mt_arrived(copies):
        @pl.when(has_r)
        def _():
            for copy in copies:
                copy.wait_recv()

    def row_step(u):
        row_first(u)
        mt_arrived(mt_downs(u))
        row_own(u, 0, nblk)
        row_rows(u, 0, steps)
        send_c2(u)

    def plan_step(u):
        @pl.when(has_l)
        def _():
            c2_up(u).wait_recv()

        @pl.when(has_r)
        def _():
            c2_down(u).wait_recv()

        transport(u)
        for cond, _, copy in line_copies(u):
            @pl.when(cond)
            def _():
                copy.start()

    def wait_slots(slots, edges):
        for _, cond, copy in line_copies(None, slots, edges):
            @pl.when(cond)
            def _():
                copy.wait_recv()

    part = wide // 3 if (wide // 3) % 16 == 0 else wide
    step_rows = 96

    def conv_pair(src, k, slot, store, new_slots=()):
        count = wide // part
        for i in range(count):
            if i == 1 and new_slots:
                wait_slots(new_slots, True)
            g = (i + count // 2) % count
            rows = slice(g * part, (g + 1) * part)
            ins = jnp.concatenate([src[slot - 1 + i, rows, :] for i in range(4)], axis=1)
            y = jnp.dot(ins, wbig[k], preferred_element_type=F32)
            for j in range(6):
                y_ref[j, 8 + g * part : 8 + (g + 1) * part, :] = y[:, j * chans : (j + 1) * chans]
        for h in range(2):
            store(h, src, slot + h, bias_ref[k : k + 1, :])

    def updated(h, src, slot, bias, at, rows):
        total = (
            y_ref[3 * h, 7 + at : 7 + at + rows, :]
            + y_ref[3 * h + 1, 8 + at : 8 + at + rows, :]
            + y_ref[3 * h + 2, 9 + at : 9 + at + rows, :]
        )
        state = src[slot, at : at + rows, :].astype(F32)
        return (state + jnp.maximum(total + bias, 0.0)).astype(BF16)

    def clear_edges(dst, first, last):
        @pl.when(jnp.logical_not(has_l))
        def _():
            dst[first:last, 0:PAD, :] = jnp.zeros((last - first, PAD, chans), BF16)

        @pl.when(jnp.logical_not(has_r))
        def _():
            dst[first:last, n + PAD : wide, :] = jnp.zeros((last - first, PAD, chans), BF16)

        if first < REACH:
            stop = min(last, REACH)

            @pl.when(jnp.logical_not(has_x))
            def _():
                dst[first:stop] = jnp.zeros((stop - first, wide, chans), BF16)

    def layer_pair(src, dst, k, first, new_slots=()):
        wait_slots(new_slots, False)

        def keep(h, src, slot, bias):
            for at in range(0, wide, step_rows):
                dst[slot, at : at + step_rows, :] = updated(h, src, slot, bias, at, step_rows)

        conv_pair(src, k, first, keep, new_slots)
        clear_edges(dst, first, first + 2)

    def line_out(u):
        return pltpu.make_async_copy(out_ref.at[u], out_hbm.at[line_of(u)], out_sem.at[u])

    def put(h, src, slot, bias):
        for at in range(0, n, 128):
            out_ref[slot - REACH, at : at + 128, :] = updated(h, src, slot, bias, at + PAD, 128)
        line_out(slot - REACH).start()

    scores_step(0)
    send_halo(1, 1)
    send_halo(2, 0)
    scores_step(1)
    send_halo(2, 1)
    row_step(0)
    send_halo(3, 0)
    scores_step(2)
    send_halo(3, 1)
    row_step(1)
    plan_step(0)
    scores_step(3)
    row_step(2)
    plan_step(1)
    per = blk // rows_at
    row_first(last)
    mt_arrived(mt_downs(last)[:-1])
    row_own(last, 0, nblk - 1)
    row_rows(last, 0, steps - per)
    mt_arrived(mt_downs(last)[-1:])
    row_own(last, nblk - 1, nblk)
    if per == 1:
        col_sum(last, steps - 1, row_exp(last, steps - 1, row_max(last, steps - 1)))
    else:
        row_rows(last, steps - per, steps)
    send_c2(last)
    plan_step(2)
    plan_step(3)
    disp_out = pltpu.make_async_copy(disp_ref, disp_hbm, out_sem.at[lines])
    disp_out.start()
    layer_pair(x0, x1, 0, 3, (2, 3, 4, 5))
    layer_pair(x0, x1, 0, 1, (0, 1))
    layer_pair(x1, x2, 1, 2)
    layer_pair(x0, x1, 0, 5, (6, 7))
    layer_pair(x0, x1, 0, 7, (8, 9))
    layer_pair(x1, x2, 1, 4)
    layer_pair(x1, x2, 1, 6)
    conv_pair(x2, 2, 3, put)
    conv_pair(x2, 2, 5, put)
    disp_out.wait()
    for u in range(lines):
        line_out(u).wait()

    @pl.when(has_r)
    def _():
        for u in range(lines):
            for copy in halo_copies(u):
                copy.wait_send()
            mt_up(u).wait_send()
            c2_up(u).wait_send()

    @pl.when(has_l)
    def _():
        for u in range(lines):
            for copy in mt_downs(u):
                copy.wait_send()
            c2_down(u).wait_send()

    for cond, _, copy in line_copies(None):
        @pl.when(cond)
        def _():
            copy.wait_send()


def hand_over(pieces, src, disp_src, dst, disp_dst, hold, disp_hold, in_sem, out_sem):
    lines, n, _ = src.shape
    size = lines * n // pieces
    spots = [(k * size // n, pl.ds(k * size % n, size)) for k in range(pieces)]
    loads = [
        pltpu.make_async_copy(src.at[at], hold.at[at], in_sem.at[k]) for k, at in enumerate(spots)
    ]
    stores = [
        pltpu.make_async_copy(hold.at[at], dst.at[at], out_sem.at[k]) for k, at in enumerate(spots)
    ]
    loads.append(pltpu.make_async_copy(disp_src, disp_hold, in_sem.at[pieces]))
    stores.append(pltpu.make_async_copy(disp_hold, disp_dst, out_sem.at[pieces]))
    for load in loads:
        load.start()
    for load, store in zip(loads, stores):
        load.wait()
        store.start()
    for store in stores:
        store.wait()


def shards(segs, line_devs, left, right, weight, bias):
    lines, n, chans = left.shape
    layers = weight.shape[0]
    blk = n // 4
    wide = n + 2 * PAD
    slots = lines + 2 * REACH
    shape = (segs, line_devs, lines, n, blk, chans, layers)
    dma = pltpu.SemaphoreType.DMA
    vm = pltpu.VMEM
    refined, disparity = pl.pallas_call(
        functools.partial(body, shape),
        out_shape=(
            jax.ShapeDtypeStruct((lines, n, chans), BF16),
            jax.ShapeDtypeStruct((lines, n), F32),
        ),
        in_specs=[pl.BlockSpec(memory_space=pl.ANY)] * 3 + [pl.BlockSpec(memory_space=vm)],
        out_specs=(pl.BlockSpec(memory_space=pl.ANY), pl.BlockSpec(memory_space=pl.ANY)),
        scratch_shapes=[
            vm((lines, n, chans), BF16),
            vm((lines, 2 * n, chans), BF16),
            vm((2 * n, chans), BF16),
            vm((lines, n, n + blk), F32),
            vm((3, n, n + blk), F32),
            vm((lines, 2, n), F32),
            vm((lines, 2, n), F32),
            vm((lines, 2, n), F32),
            vm((lines, 2, n), F32),
            vm((8, 2 * n), F32),
            vm((8, 2 * n), F32),
            vm((lines, 1, n), F32),
            vm((lines, 1, n), F32),
            vm((lines, 1, n), F32),
            vm((lines, 1, n), F32),
            vm(weight.shape, BF16),
            vm((layers, 4 * chans, 6 * chans), BF16),
            vm((slots, wide, chans), BF16),
            vm((slots, wide, chans), BF16),
            vm((slots, wide, chans), BF16),
            vm((6, wide + 16, chans), F32),
            dma((lines, 2)),
            dma,
            dma((lines, 4)),
            dma((lines, 4)),
            dma((lines + 4, 2)),
            dma((lines + 4, 2)),
            dma((lines, 2)),
            dma((lines, 2)),
            dma((lines, 3, 3)),
            dma((slots, 3)),
            vm((lines, n, chans), BF16),
            vm((lines, n), F32),
            dma((lines + 1,)),
        ],
        compiler_params=pltpu.CompilerParams(
            collective_id=0, has_side_effects=True, vmem_limit_bytes=60 * 1024 * 1024
        ),
        name="stereo",
    )(left, right, weight, bias)
    pieces = 8
    return pl.pallas_call(
        functools.partial(hand_over, pieces),
        out_shape=(
            jax.ShapeDtypeStruct((lines, n, chans), BF16),
            jax.ShapeDtypeStruct((lines, n), F32),
        ),
        in_specs=[pl.BlockSpec(memory_space=pl.ANY)] * 2,
        out_specs=(pl.BlockSpec(memory_space=pl.ANY), pl.BlockSpec(memory_space=pl.ANY)),
        scratch_shapes=[
            vm((lines, n, chans), BF16),
            vm((lines, n), F32),
            dma((pieces + 1,)),
            dma((pieces + 1,)),
        ],
        name="hand_over",
    )(refined, disparity)


def solution(mesh):
    return jax.shard_map(
        functools.partial(shards, mesh.shape["seg"], mesh.shape["lines"]),
        mesh=mesh,
        in_specs=(P("lines", "seg", None), P("lines", "seg", None), P(), P()),
        out_specs=(P("lines", "seg", None), P("lines", "seg")),
        check_vma=False,
    )
```
